32 devices in a mesh: grp: 2 (over y), frm: 4 (over z), row: 4 (over x, core).
Axes of the slice: x: 2, y: 2, z: 4, core: 2. Of those that a mesh axis runs over, the one named last changes fastest.
Arguments:
- hidden_in: bfloat16 [512, 16, 2240], P('row', ('grp', 'frm')), parts along dimension 1, may hold values from -6 to 6
- norm_gain: float32 [2240], replicated, may hold values from 0.1 to 1.9
- query_key_value_weight: bfloat16 [2240, 3, 2240], P(None, None, 'row'), may hold values from -0.125 to 0.125
- head_gain: float32 [2240], P('row'), may hold values from 0.1 to 1.9
- output_matrix: bfloat16 [2240, 2240], P('row'), may hold values from -0.125 to 0.125
- block_end: int32 [16], P(('grp', 'frm')), parts along dimension 0, may hold values from 0 to 7, as said below
Outputs:
- mixed_out: bfloat16 [512, 16, 2240], P('row', ('grp', 'frm')), parts along dimension 1
The draws below stay inside these ranges and needn't reach their ends.
There are 2 independent parts, one for each index of `grp`. The reference program is written for one: setup_inputs(seed, part) draws one part's arguments, and reference() takes and returns one part's arrays. A program takes and returns all parts, laid end to end along the dimension named above; an argument that names none is the same for every part. Nothing has to cross between parts.
Inputs may be any that keep to these rules, and one draw needn't show every extreme that they name: `block_end`: entries never fall from one frame to the next; each entry is at least its frame's index, and frames with equal entries form a block of consecutive frames; a block never holds frames of two different runs of 2 frames (f // 2 differs), and the last frame of every such run ends a block.
All inputs are finite; a program needn't handle non-finite values.
Results may differ from the reference program's by a relative error of at most 0.015.
Values may be sent and summed in bfloat16 or wider, within the bound.
No kernel may reach another device: no remote copies, remote signals or barrier semaphores. Data moves between devices by JAX's collectives and lax.ppermute only.
A program may use at most 64 MiB of HBM per device.

```python
import jax
import jax.numpy as jnp
from jax import lax

D = 2240
HEADS = 20
HD = 112
FH = 16
FW = 32
FR_DEV = 2
FRAMES = 8
N_ROW = 4


def draw_block_end(key, part):
    frame_index = jnp.arange(FRAMES, dtype=jnp.int32)
    coins = jax.random.randint(jax.random.fold_in(key, 7), (FRAMES,), 0, 2, dtype=jnp.int32)
    starts = jnp.where(frame_index % FR_DEV == 0, 1, coins)
    block_ident = jnp.cumsum(starts) - 1
    same_block = block_ident[None, :] == block_ident[:, None]
    return jnp.max(jnp.where(same_block, frame_index[None, :], -1), axis=1).astype(jnp.int32)


def level_of(key, dims, split, smallest, high):
    factor_of = 1.0
    for dim, blocks in split:
        heights = jax.random.uniform(jax.random.fold_in(jax.random.fold_in(key, 6), dim), (blocks,), jnp.float32, smallest / len(split), high / len(split))
        factor_of = factor_of * jnp.repeat(jnp.exp(heights), dims[dim] // blocks).reshape((-1,) + (1,) * (len(dims) - 1 - dim))
    return factor_of


def noise(stream_key, extent, width, most, split=(), kind=jnp.bfloat16):
    drawn = jax.random.normal(stream_key, extent, jnp.float32) * width
    if len(split) > 0:
        drawn = level_of(stream_key, extent, split, -0.22, 0.18) * drawn
    return jnp.clip(drawn, min=-most, max=most).astype(kind)


def setup_inputs(seed: int = 0, part: int = 0) -> dict:
    seeds = jax.random.split(jax.random.key(seed), 7)
    own_keys = jax.random.split(jax.random.fold_in(seeds[6], part), 7)
    return {
        "hidden_in": noise(own_keys[0], (FH * FW, FRAMES, D), 1.0, 6.0, ((0, 4), (1, 4))),
        "norm_gain": jnp.clip(1.0 + 0.18 * jax.random.normal(seeds[1], (D,), jnp.float32), 0.1, 1.9),
        "query_key_value_weight": noise(seeds[2], (D, 3, HEADS * HD), D ** -0.5, 0.125, ((2, 4),)),
        "head_gain": jnp.clip(1.0 + 0.18 * jax.random.normal(seeds[3], (HEADS * HD,), jnp.float32), 0.1, 1.9),
        "output_matrix": noise(seeds[4], (HEADS * HD, D), (HEADS * HD) ** -0.5, 0.125, ((0, 4),)),
        "block_end": draw_block_end(jax.random.fold_in(jax.random.fold_in(seeds[6], part), 71), part),
    }


epsilon = 1e-06

def reference(hidden_in, norm_gain, query_key_value_weight, head_gain, output_matrix, block_end):
    positions = FH * FW
    as_float = hidden_in.astype(jnp.float32)
    mean_square = lax.optimization_barrier(jnp.mean(as_float * as_float, axis=-1, keepdims=True))
    normed = (as_float * lax.rsqrt(mean_square + epsilon) * norm_gain).astype(jnp.bfloat16)
    weights = query_key_value_weight.reshape(D, 3 * HEADS * HD)
    projected = jnp.dot(normed.reshape(positions * FRAMES, D), weights, preferred_element_type=jnp.float32).astype(jnp.bfloat16)
    projected = projected.reshape(positions, FRAMES, 3, HEADS, HD)
    queries = jax.nn.relu(projected[:, :, 0]).astype(jnp.float32)
    key_relu = jax.nn.relu(projected[:, :, 1]).astype(jnp.float32)
    values = projected[:, :, 2].astype(jnp.float32)
    per_frame_state = jnp.einsum('pfhi,pfhj->fhij', key_relu, values, precision=lax.Precision.HIGHEST)
    earlier_mask = (block_end[None, :] <= block_end[:, None]).astype(jnp.float32)
    block_state = jnp.einsum('fg,ghij->fhij', earlier_mask, per_frame_state, precision=lax.Precision.HIGHEST).astype(jnp.bfloat16)
    attended = jnp.einsum('pfhi,fhij->pfhj', queries, block_state.astype(jnp.float32), precision=lax.Precision.HIGHEST)
    head_square = lax.optimization_barrier(jnp.mean(attended * attended, axis=-1, keepdims=True))
    head_out = (attended * lax.rsqrt(head_square + epsilon) * head_gain.reshape(HEADS, HD)).astype(jnp.bfloat16)
    merged_heads = head_out.reshape(positions * FRAMES, HEADS * HD)
    group_width = HEADS * HD // N_ROW
    summed = jnp.zeros((positions * FRAMES, D), jnp.float32)
    for group in range(N_ROW):
        head_cols = merged_heads[:, group * group_width:(group + 1) * group_width]
        weight_part = output_matrix[group * group_width:(group + 1) * group_width]
        partial_term = jnp.dot(head_cols, weight_part, preferred_element_type=jnp.float32)
        rounded = lax.optimization_barrier(partial_term.astype(jnp.bfloat16)).astype(jnp.float32)
        summed = summed + rounded
    return summed.astype(jnp.bfloat16).reshape(positions, FRAMES, D)
```

```python
import functools

import jax
import jax.numpy as jnp
from jax import lax
from jax.experimental import pallas as pl
from jax.experimental.pallas import tpu as pltpu
from jax.sharding import PartitionSpec as P

HD = 112
EPS = 1e-06
F32 = jnp.float32
BF16 = jnp.bfloat16


def whole(shape):
    return pl.BlockSpec(shape, lambda *g: (0,) * len(shape))


def cost(flops, nbytes):
    return pl.CostEstimate(flops=int(flops), bytes_accessed=int(nbytes), transcendentals=0)


def params(mib=48):
    return pltpu.CompilerParams(vmem_limit_bytes=mib << 20)


def dot(a, b):
    return jnp.dot(a, b, preferred_element_type=F32)


def dot_nt(a, b):
    return lax.dot_general(a, b, (((1,), (1,)), ((), ())), preferred_element_type=F32)


def project_kernel(shape, refs, gain_ref, w_ref, outs, scratch):
    frames, per_frame, lanes, heads, with_query = shape
    normed, keys = scratch
    state_ref = outs[0]
    step = pl.program_id(0)
    width = per_frame * lanes

    @pl.when(step == 0)
    def _():
        for f in range(frames):
            for b in range(per_frame):
                x = refs[f][b][...].astype(F32)
                mean = jnp.mean(x * x, axis=0, keepdims=True)
                at = (f * per_frame + b) * lanes
                normed[:, at : at + lanes] = (x * lax.rsqrt(mean + EPS) * gain_ref[...]).astype(BF16)
        keys[...] = jnp.maximum(dot(w_ref[0], normed[...]), 0.0).astype(BF16)

    @pl.when(step == 1)
    def _():
        values = dot(w_ref[0], normed[...]).astype(BF16)
        for f in range(frames):
            cols = slice(f * width, (f + 1) * width)
            for h in range(heads):
                rows = slice(h * HD, (h + 1) * HD)
                state_ref[f, rows, :] = dot_nt(values[rows, cols], keys[rows, cols])

    if with_query:

        @pl.when(step == 2)
        def _():
            q = jnp.maximum(dot(w_ref[0], normed[...]), 0.0).astype(BF16)
            for f in range(frames):
                outs[1][f] = q[:, f * width : (f + 1) * width]


def project(tokens, gain, weights, with_query=True):
    frames, per_frame = len(tokens), len(tokens[0])
    flat = [t for row in tokens for t in row]
    features, lanes = flat[0][0].shape[-2:]
    group = weights.shape[1]
    heads = group // HD
    total = frames * per_frame * lanes
    shape = (frames, per_frame, lanes, heads, with_query)
    steps = 3 if with_query else 2

    specs = []
    for array, index in flat:
        if index is None:
            specs.append(whole((features, lanes)))
        else:
            specs.append(pl.BlockSpec((None, features, lanes), lambda g, i=index: (i, 0, 0)))
    out_shape = [jax.ShapeDtypeStruct((frames, group, HD), F32)]
    out_specs = [whole((frames, group, HD))]
    if with_query:
        out_shape.append(jax.ShapeDtypeStruct((frames, group, per_frame * lanes), BF16))
        out_specs.append(whole((frames, group, per_frame * lanes)))
    n_tokens, n_out = len(flat), len(out_shape)

    def kernel(*refs):
        blocks = refs[:n_tokens]
        gain_ref, w_ref = refs[n_tokens : n_tokens + 2]
        outs = refs[n_tokens + 2 : n_tokens + 2 + n_out]
        scratch = refs[n_tokens + 2 + n_out :]
        rows = [blocks[f * per_frame : (f + 1) * per_frame] for f in range(frames)]
        project_kernel(shape, rows, gain_ref, w_ref, outs, scratch)

    out = pl.pallas_call(
        kernel,
        grid=(steps,),
        in_specs=specs
        + [
            whole((features, 1)),
            pl.BlockSpec((1, group, features), lambda g: ((g + 1) % 3, 0, 0)),
        ],
        out_specs=out_specs,
        out_shape=out_shape,
        scratch_shapes=[pltpu.VMEM((features, total), BF16), pltpu.VMEM((group, total), BF16)],
        compiler_params=params(),
        cost_estimate=cost(2 * steps * group * features * total, 2 * steps * group * features),
        name="project",
    )(*[a for a, _ in flat], gain, weights)
    return out


def query_kernel(n, gain_ref, w_ref, blocks, q_ref, normed):
    lanes = blocks[0].shape[-1]
    for b in range(n):
        x = blocks[b][...].astype(F32)
        mean = jnp.mean(x * x, axis=0, keepdims=True)
        normed[:, b * lanes : (b + 1) * lanes] = (
            x * lax.rsqrt(mean + EPS) * gain_ref[...]
        ).astype(BF16)
    q_ref[0] = jnp.maximum(dot(w_ref[0], normed[...]), 0.0).astype(BF16)


def query(blocks, gain, weights):
    n = len(blocks)
    features, lanes = blocks[0].shape
    group = weights.shape[1]

    def kernel(gain_ref, w_ref, *rest):
        query_kernel(n, gain_ref, w_ref, rest[:n], rest[n], rest[n + 1])

    return pl.pallas_call(
        kernel,
        grid=(1,),
        in_specs=[whole((features, 1)), whole((1, group, features))] + [whole((features, lanes))] * n,
        out_specs=whole((1, group, n * lanes)),
        out_shape=jax.ShapeDtypeStruct((1, group, n * lanes), BF16),
        scratch_shapes=[pltpu.VMEM((features, n * lanes), BF16)],
        compiler_params=params(),
        cost_estimate=cost(2 * group * features * n * lanes, 2 * group * features),
        name="query",
    )(gain, weights, *blocks)


def attend(end, states, priors, head_gain, queries, lanes):
    frames, group, _ = states.shape
    heads = group // HD
    n_prior, n_q = len(priors), len(queries)
    places, slabs = [], 0
    seen = {}
    for k, (array, where, first) in enumerate(queries):
        for f, i in where.items():
            for b in range(array.shape[-1] // lanes):
                places.append((k, f, i, b, first + b))
                seen[first + b] = True
    slabs = len(seen)

    def kernel(end_ref, state_ref, gain_ref, *rest):
        prior_refs, q_refs = rest[:n_prior], rest[n_prior : n_prior + n_q]
        outs = rest[n_prior + n_q :]
        prior = jnp.zeros((group, HD), F32)
        for p in prior_refs:
            prior = prior + p[...].astype(F32)
        block = []
        for f in range(frames):
            total = prior
            for g in range(frames):
                seen_by = (end_ref[g] <= end_ref[f]).astype(F32)
                total = total + seen_by * state_ref[g]
            block.append(total.astype(BF16))
        for k, f, i, b, slab in places:
            for h in range(heads):
                rows = slice(h * HD, (h + 1) * HD)
                a = dot(block[f][rows], q_refs[k][i, rows, b * lanes : (b + 1) * lanes])
                mean = jnp.mean(a * a, axis=0, keepdims=True)
                outs[slab][f, rows, :] = (a * lax.rsqrt(mean + EPS) * gain_ref[rows]).astype(BF16)

    return pl.pallas_call(
        kernel,
        in_specs=[pl.BlockSpec(memory_space=pltpu.SMEM)]
        + [pl.BlockSpec(memory_space=pltpu.VMEM)] * (2 + n_prior + n_q),
        out_specs=[pl.BlockSpec(memory_space=pltpu.VMEM)] * slabs,
        out_shape=[jax.ShapeDtypeStruct((frames, group, lanes), BF16)] * slabs,
        compiler_params=params(),
        cost_estimate=cost(2 * group * HD * frames * slabs * lanes, 4 * group * frames * slabs * lanes),
        name="attend",
    )(end, states, head_gain, *priors, *[a for a, _, _ in queries])


def mix(weights, heads_out, part, parts, dtype):
    n = len(weights)
    width, group = weights[0].shape
    frames, _, lanes = heads_out[0].shape
    rows = width // parts

    def kernel(*refs):
        total = None
        for w, x in zip(refs[:n], refs[n : 2 * n]):
            cols = jnp.concatenate([x[f] for f in range(frames)], axis=1)
            term = dot(w[...], cols)
            total = term if total is None else total + term
        for f in range(frames):
            refs[2 * n][f] = total[:, f * lanes : (f + 1) * lanes].astype(dtype)

    return pl.pallas_call(
        kernel,
        grid=(1,),
        in_specs=[pl.BlockSpec((rows, group), lambda g: (part, 0))] * n
        + [whole((frames, group, lanes))] * n,
        out_specs=whole((frames, rows, lanes)),
        out_shape=jax.ShapeDtypeStruct((frames, rows, lanes), dtype),
        compiler_params=params(),
        cost_estimate=cost(2 * n * rows * group * frames * lanes, 2 * n * rows * group),
        name="mix",
    )(*weights, *heads_out)


PARTS = 2


def per_device(n_row, n_frm, hidden_in, norm_gain, qkv_weight, head_gain, output_matrix, block_end):
    def swap(v, k):
        return lax.ppermute(v, "row", [(i, i ^ k) for i in range(n_row)])

    def shift(v, s):
        return lax.ppermute(v, "frm", [(i, i + s) for i in range(n_frm - s)])

    lanes, frames, features = hidden_in.shape
    tokens = jnp.transpose(hidden_in, (1, 2, 0))
    weights = jnp.transpose(qkv_weight, (1, 2, 0))
    gain = norm_gain.reshape(features, 1)
    out_gain = head_gain.reshape(-1, 1)

    pairs = n_row // 2
    crossed = {}
    for f in range(frames):
        for k in range(1, pairs):
            crossed[k, f] = swap(tokens[f], 2 * k)
    sibling = swap(tokens, 1)
    passed = {key: swap(v, 1) for key, v in crossed.items()}

    mix_own = jnp.transpose(output_matrix)
    mix_sibling = swap(mix_own, 1)

    near, near_q = project([[(tokens, f), (sibling, f)] for f in range(frames)], gain, weights)
    states = near
    far_q = []
    late = []
    for f in range(frames):
        for k in range(1, pairs):
            blocks = [crossed[k, f], passed[k, f]]
            last = f == frames - 1 and k == pairs - 1
            out = project([[(b, None) for b in blocks]], gain, weights, not last)
            states = states + jnp.zeros_like(states).at[f].set(out[0][0])
            if last:
                late.append((f, k, blocks))
            else:
                far_q.append((out[1], {f: 0}, 2 * k))
    own_sum = jnp.sum(states, axis=0).astype(BF16)
    if n_frm <= 4:
        priors = [shift(own_sum, s) for s in range(1, n_frm)]
    else:
        total, s = shift(own_sum.astype(F32), 1), 1
        while s < n_frm:
            total, s = total + shift(total, s), 2 * s
        priors = [total]
    for f, k, blocks in late:
        far_q.append((query(blocks, gain, weights), {f: 0}, 2 * k))

    queries = far_q + [(near_q, {f: f for f in range(frames)}, 0)]
    heads_out = attend(block_end, states, priors, out_gain, queries, lanes)

    got = {}
    for k in list(range(1, pairs)) + [0]:
        got[k] = swap(heads_out[2 * k + 1], 1)
    both = (mix_own, mix_sibling)
    arrived = []
    for part in range(PARTS):
        arrived.append(
            [
                swap(mix(both, (heads_out[2 * k], got[k]), part, PARTS, BF16), 2 * k)
                for k in range(1, pairs)
            ]
        )
    done = []
    for part in range(PARTS):
        total = mix(both, (heads_out[0], got[0]), part, PARTS, F32)
        for v in arrived[part]:
            total = total + v.astype(F32)
        done.append(total.astype(BF16))
    return jnp.transpose(jnp.concatenate(done, axis=1), (2, 0, 1))


def solution(mesh):
    placed = (
        P("row", ("grp", "frm"), None),
        P(),
        P(None, None, "row"),
        P("row"),
        P("row", None),
        P(("grp", "frm")),
    )
    return jax.shard_map(
        functools.partial(per_device, mesh.shape["row"], mesh.shape["frm"]),
        mesh=mesh,
        in_specs=placed,
        out_specs=P("row", ("grp", "frm"), None),
        check_vma=False,
    )
```

```python
import jax
import jax.numpy as jnp
from jax import lax
from jax.experimental import pallas as pl
from jax.experimental.pallas import tpu as pltpu
from jax.sharding import PartitionSpec as P


HD = 112
EPS = 1e-06
F32 = jnp.float32
BF16 = jnp.bfloat16


def cost(flops, nbytes):
    return pl.CostEstimate(flops=int(flops), bytes_accessed=int(nbytes), transcendentals=0)


def params(mib=48):
    return pltpu.CompilerParams(vmem_limit_bytes=mib << 20)


def dot(a, b):
    return jnp.dot(a, b, preferred_element_type=F32)


def dot_nt(a, b):
    return lax.dot_general(a, b, (((1,), (1,)), ((), ())), preferred_element_type=F32)


VMEM = pl.BlockSpec(memory_space=pltpu.VMEM)


def scaled(x_ref, gain_ref):
    x = x_ref[...].astype(F32)
    mean = jnp.mean(x * x, axis=0, keepdims=True)
    return (x * lax.rsqrt(mean + EPS) * gain_ref[...]).astype(BF16)


def project(blocks, where, gain, weights, states=None, frames=1, first=0, last=False):
    n = len(blocks)
    here, per_frame = len(where), len(where[0])
    features, lanes = blocks[0].shape[-2:]
    group = weights.shape[0] // 3
    heads = group // HD
    width = per_frame * lanes
    total = here * width
    begin = group if last else 0

    def kernel(*refs):
        x_refs, rest = refs[:n], refs[n:]
        gain_ref, w_ref, rest = rest[0], rest[1], rest[2:]
        if states is not None:
            old, rest = rest[0], rest[1:]
        state, second, normed, part = rest[0], rest[1], rest[-2], rest[-1]
        if last:
            normed = rest[2]
        for f in range(here):
            for b, (k, i) in enumerate(where[f]):
                block = x_refs[k] if i is None else x_refs[k].at[i]
                at = f * width + b * lanes
                normed[:, at : at + lanes] = scaled(block, gain_ref)
        part[...] = jnp.dot(w_ref[begin:, :], normed[...], preferred_element_type=F32).astype(BF16)
        keys, values = group - begin, 2 * group - begin
        for f in range(here):
            cols = slice(f * width, (f + 1) * width)
            for h in range(heads):
                k = jnp.maximum(part[keys + h * HD : keys + (h + 1) * HD, cols], 0.0)
                v = part[values + h * HD : values + (h + 1) * HD, cols]
                rows = slice(h * HD, (h + 1) * HD)
                add = dot_nt(v, k)
                state[first + f, rows, :] = add if states is None else old[first + f, rows, :] + add
        if states is not None:
            for f in range(frames):
                if not first <= f < first + here:
                    state[f] = old[f]
        if last:
            own = state[0]
            for f in range(1, frames):
                own = own + state[f]
            second[...] = own.astype(BF16)
        else:
            for f in range(here):
                second[f] = jnp.maximum(part[:group, f * width : (f + 1) * width], 0.0)

    out_shape = [jax.ShapeDtypeStruct((frames, group, HD), F32)]
    scratch = [pltpu.VMEM((3 * group - begin, total), BF16)]
    if last:
        out_shape.append(jax.ShapeDtypeStruct((group, HD), BF16))
        out_shape.append(jax.ShapeDtypeStruct((features, total), BF16))
    else:
        out_shape.append(jax.ShapeDtypeStruct((here, group, width), BF16))
        scratch = [pltpu.VMEM((features, total), BF16)] + scratch
    given = [*blocks, gain, weights] + ([] if states is None else [states])
    return pl.pallas_call(
        kernel,
        in_specs=[VMEM] * len(given),
        out_specs=[VMEM] * len(out_shape),
        out_shape=out_shape,
        scratch_shapes=scratch,
        compiler_params=params(),
        cost_estimate=cost(2 * (3 * group - begin) * features * total, 2 * features * total),
        name="project",
    )(*given)


def query(normed, weights):
    features, total = normed.shape
    group = weights.shape[0] // 3

    def kernel(x_ref, w_ref, q_ref):
        q_ref[0] = jnp.maximum(dot(w_ref[:group, :], x_ref[...]), 0.0).astype(BF16)

    return pl.pallas_call(
        kernel,
        in_specs=[VMEM] * 2,
        out_specs=VMEM,
        out_shape=jax.ShapeDtypeStruct((1, group, total), BF16),
        compiler_params=params(),
        cost_estimate=cost(2 * group * features * total, 2 * features * total),
        name="query",
    )(normed, weights)


def attend(end, states, priors, head_gain, queries, lanes):
    frames, group, _ = states.shape
    heads = group // HD
    n_prior, n_q = len(priors), len(queries)
    places, slabs = [], 0
    seen = {}
    for k, (array, where, first) in enumerate(queries):
        for f, i in where.items():
            for b in range(array.shape[-1] // lanes):
                places.append((k, f, i, b, first + b))
                seen[first + b] = True
    slabs = len(seen)

    def kernel(end_ref, state_ref, gain_ref, *rest):
        prior_refs, q_refs = rest[:n_prior], rest[n_prior : n_prior + n_q]
        outs = rest[n_prior + n_q :]
        prior = jnp.zeros((group, HD), F32)
        for p in prior_refs:
            prior = prior + p[...].astype(F32)
        block = []
        for f in range(frames):
            total = prior
            for g in range(frames):
                seen_by = (end_ref[g] <= end_ref[f]).astype(F32)
                total = total + seen_by * state_ref[g]
            block.append(total.astype(BF16))
        for k, f, i, b, slab in places:
            for h in range(heads):
                rows = slice(h * HD, (h + 1) * HD)
                a = dot(block[f][rows], q_refs[k][i, rows, b * lanes : (b + 1) * lanes])
                mean = jnp.mean(a * a, axis=0, keepdims=True)
                outs[slab][f, rows, :] = (a * lax.rsqrt(mean + EPS) * gain_ref[rows]).astype(BF16)

    return pl.pallas_call(
        kernel,
        in_specs=[pl.BlockSpec(memory_space=pltpu.SMEM)]
        + [pl.BlockSpec(memory_space=pltpu.VMEM)] * (2 + n_prior + n_q),
        out_specs=[pl.BlockSpec(memory_space=pltpu.VMEM)] * slabs,
        out_shape=[jax.ShapeDtypeStruct((frames, group, lanes), BF16)] * slabs,
        compiler_params=params(),
        cost_estimate=cost(2 * group * HD * frames * slabs * lanes, 4 * group * frames * slabs * lanes),
        name="attend",
    )(end, states, head_gain, *priors, *[a for a, _, _ in queries])


def turn(pieces):
    n = len(pieces)
    group, width = pieces[0].shape

    def kernel(*refs):
        for k in range(n):
            refs[n][:, k * group : (k + 1) * group] = refs[k][...].T

    return pl.pallas_call(
        kernel,
        in_specs=[VMEM] * n,
        out_specs=VMEM,
        out_shape=jax.ShapeDtypeStruct((width, n * group), BF16),
        compiler_params=params(),
        cost_estimate=cost(0, 4 * n * group * width),
        name="turn",
    )(*pieces)


def mix(weights, heads_out, start, stop, dtype):
    n = len(heads_out)
    frames, group, lanes = heads_out[0].shape

    def kernel(w_ref, *refs):
        out, both = refs[n], refs[n + 1]
        for k in range(n):
            for f in range(frames):
                both[k * group : (k + 1) * group, f * lanes : (f + 1) * lanes] = refs[k][f]
        total = dot(w_ref[start:stop, :], both[...])
        for f in range(frames):
            out[f] = total[:, f * lanes : (f + 1) * lanes].astype(dtype)

    return pl.pallas_call(
        kernel,
        in_specs=[VMEM] * (1 + n),
        out_specs=VMEM,
        out_shape=jax.ShapeDtypeStruct((frames, stop - start, lanes), dtype),
        scratch_shapes=[pltpu.VMEM((n * group, frames * lanes), BF16)],
        compiler_params=params(),
        cost_estimate=cost(2 * n * (stop - start) * group * frames * lanes, 2 * n * (stop - start) * group),
        name="mix",
    )(weights, *heads_out)


def finish(buffer, own, arrived, start, whole_shape):
    n = len(arrived)
    frames, rows, lanes = arrived[0].shape

    def kernel(*refs):
        own_ref, got, out, staged, sem = refs[0], refs[1 : 1 + n], refs[-3], refs[-2], refs[-1]
        copies = []
        for f in range(frames):
            total = own_ref[f, start : start + rows, :]
            for g in got:
                total = total + g[f].astype(F32)
            staged[f] = total.astype(BF16)
            copies.append(pltpu.make_async_copy(staged.at[f], out.at[f, pl.ds(start, rows), :], sem.at[f]))
            copies[-1].start()
        for c in copies:
            c.wait()

    given = [own, *arrived] + ([] if buffer is None else [buffer])
    return pl.pallas_call(
        kernel,
        in_specs=[VMEM] * (1 + n) + ([] if buffer is None else [pl.BlockSpec(memory_space=pl.ANY)]),
        out_specs=pl.BlockSpec(memory_space=pl.ANY),
        out_shape=jax.ShapeDtypeStruct(whole_shape, BF16),
        scratch_shapes=[pltpu.VMEM((frames, rows, lanes), BF16), pltpu.SemaphoreType.DMA((frames,))],
        input_output_aliases={} if buffer is None else {1 + n: 0},
        compiler_params=params(),
        cost_estimate=cost(0, 8 * frames * rows * lanes),
        name="finish",
    )(*given)


CUTS = (0.0, 0.25, 0.75, 1.0)


def per_device(n_row, n_frm, hidden_in, norm_gain, qkv_weight, head_gain, output_matrix, block_end):
    def swap(v, k):
        return lax.ppermute(v, "row", [(i, i ^ k) for i in range(n_row)])

    def shift(v, s):
        return lax.ppermute(v, "frm", [(i, i + s) for i in range(n_frm - s)])

    lanes, frames, features = hidden_in.shape
    tokens = jnp.transpose(hidden_in, (1, 2, 0))
    weights = jnp.transpose(qkv_weight, (1, 2, 0)).reshape(-1, features)
    gain = norm_gain.reshape(features, 1)
    out_gain = head_gain.reshape(-1, 1)

    pairs = n_row // 2
    crossed = {}
    for f in range(frames):
        for k in range(1, pairs):
            crossed[k, f] = swap(tokens[f], 2 * k)
    sibling = swap(tokens, 1)
    passed = {key: swap(v, 1) for key, v in crossed.items()}

    where = [[(0, f), (1, f)] for f in range(frames)]
    states, near_q = project([tokens, sibling], where, gain, weights, None, frames)
    turned = turn([output_matrix, swap(output_matrix, 1)])
    states, turned = lax.optimization_barrier((states, turned))
    queries = []
    for f in range(frames):
        for k in range(1, pairs):
            last = f == frames - 1 and k == pairs - 1
            blocks = [crossed[k, f], passed[k, f]]
            out = project(blocks, [[(0, None), (1, None)]], gain, weights, states, frames, f, last)
            states = out[0]
            if last:
                own_sum, normed = out[1:]
            else:
                queries.append((out[1], {f: 0}, 2 * k))
    if n_frm <= 4:
        priors = [shift(own_sum, s) for s in range(1, n_frm)]
    else:
        total, s = shift(own_sum.astype(F32), 1), 1
        while s < n_frm:
            total, s = total + shift(total, s), 2 * s
        priors = [total]
    queries.append((query(normed, weights), {frames - 1: 0}, n_row - 2))
    queries.append((near_q, {f: f for f in range(frames)}, 0))
    heads_out = attend(block_end, states, priors, out_gain, queries, lanes)

    got = {}
    for k in list(range(1, pairs)) + [0]:
        got[k] = swap(heads_out[2 * k + 1], 1)
    width = output_matrix.shape[1]
    cuts = [int(c * width) // 16 * 16 for c in CUTS]
    spans = list(zip(cuts[:-1], cuts[1:]))
    arrived = []
    for i, (start, stop) in enumerate(spans):
        arrived.append([])
        for k in range(1, pairs):
            part = mix(turned, (heads_out[2 * k], got[k]), start, stop, BF16)
            arrived[i].append(swap(part, 2 * k))
    own = mix(turned, (heads_out[0], got[0]), 0, width, F32)
    out = None
    for (start, stop), parts in zip(spans, arrived):
        out = finish(out, own, parts, start, (frames, width, lanes))
    return jnp.transpose(out, (2, 0, 1))


def solution(mesh):
    placed = (
        P("row", ("grp", "frm"), None),
        P(),
        P(None, None, "row"),
        P("row"),
        P("row", None),
        P(("grp", "frm")),
    )

    def body(*args):
        return per_device(mesh.shape["row"], mesh.shape["frm"], *args)

    return jax.shard_map(
        body, mesh=mesh, in_specs=placed, out_specs=P("row", ("grp", "frm"), None), check_vma=False
    )
```

```python
import jax
import jax.numpy as jnp
from jax import lax
from jax.experimental import pallas as pl
from jax.experimental.pallas import tpu as pltpu
from jax.sharding import PartitionSpec as P


HD = 112
EPS = 1e-06
F32 = jnp.float32
BF16 = jnp.bfloat16


def cost(flops, nbytes):
    return pl.CostEstimate(flops=int(flops), bytes_accessed=int(nbytes), transcendentals=0)


def params(mib=48):
    return pltpu.CompilerParams(vmem_limit_bytes=mib << 20)


def dot(a, b):
    return jnp.dot(a, b, preferred_element_type=F32)


def dot_nt(a, b):
    return lax.dot_general(a, b, (((1,), (1,)), ((), ())), preferred_element_type=F32)


VMEM = pl.BlockSpec(memory_space=pltpu.VMEM)


def scaled(x_ref, gain_ref):
    x = x_ref[...].astype(F32)
    mean = jnp.mean(x * x, axis=0, keepdims=True)
    return (x * lax.rsqrt(mean + EPS) * gain_ref[...]).astype(BF16)


def project(blocks, where, gain, weights, states=None, frames=1, first=0, last=False):
    n = len(blocks)
    here, per_frame = len(where), len(where[0])
    features, lanes = blocks[0].shape[-2:]
    group = weights.shape[0] // 3
    heads = group // HD
    width = per_frame * lanes
    total = here * width
    begin = group if last else 0

    def kernel(*refs):
        x_refs, rest = refs[:n], refs[n:]
        gain_ref, w_ref, rest = rest[0], rest[1], rest[2:]
        if states is not None:
            old, rest = rest[0], rest[1:]
        state, second, normed, part = rest[0], rest[1], rest[-2], rest[-1]
        if last:
            normed = rest[2]
        for f in range(here):
            for b, (k, i) in enumerate(where[f]):
                block = x_refs[k] if i is None else x_refs[k].at[i]
                at = f * width + b * lanes
                normed[:, at : at + lanes] = scaled(block, gain_ref)
        part[...] = jnp.dot(w_ref[begin:, :], normed[...], preferred_element_type=F32).astype(BF16)
        keys, values = group - begin, 2 * group - begin
        for f in range(here):
            cols = slice(f * width, (f + 1) * width)
            for h in range(heads):
                k = jnp.maximum(part[keys + h * HD : keys + (h + 1) * HD, cols], 0.0)
                v = part[values + h * HD : values + (h + 1) * HD, cols]
                rows = slice(h * HD, (h + 1) * HD)
                add = dot_nt(v, k)
                state[first + f, rows, :] = add if states is None else old[first + f, rows, :] + add
        if states is not None:
            for f in range(frames):
                if not first <= f < first + here:
                    state[f] = old[f]
        if last:
            own = state[0]
            for f in range(1, frames):
                own = own + state[f]
            second[...] = own.astype(BF16)
        else:
            for f in range(here):
                second[f] = jnp.maximum(part[:group, f * width : (f + 1) * width], 0.0)

    out_shape = [jax.ShapeDtypeStruct((frames, group, HD), F32)]
    scratch = [pltpu.VMEM((3 * group - begin, total), BF16)]
    if last:
        out_shape.append(jax.ShapeDtypeStruct((group, HD), BF16))
        out_shape.append(jax.ShapeDtypeStruct((features, total), BF16))
    else:
        out_shape.append(jax.ShapeDtypeStruct((here, group, width), BF16))
        scratch = [pltpu.VMEM((features, total), BF16)] + scratch
    given = [*blocks, gain, weights] + ([] if states is None else [states])
    return pl.pallas_call(
        kernel,
        in_specs=[VMEM] * len(given),
        out_specs=[VMEM] * len(out_shape),
        out_shape=out_shape,
        scratch_shapes=scratch,
        compiler_params=params(),
        cost_estimate=cost(2 * (3 * group - begin) * features * total, 2 * features * total),
        name="project",
    )(*given)


def query(normed, weights):
    features, total = normed.shape
    group = weights.shape[0] // 3

    def kernel(x_ref, w_ref, q_ref):
        q_ref[0] = jnp.maximum(dot(w_ref[:group, :], x_ref[...]), 0.0).astype(BF16)

    return pl.pallas_call(
        kernel,
        in_specs=[VMEM] * 2,
        out_specs=VMEM,
        out_shape=jax.ShapeDtypeStruct((1, group, total), BF16),
        compiler_params=params(),
        cost_estimate=cost(2 * group * features * total, 2 * features * total),
        name="query",
    )(normed, weights)


def attend(end, states, priors, head_gain, queries, lanes):
    frames, group, _ = states.shape
    heads = group // HD
    n_prior, n_q = len(priors), len(queries)
    places, slabs = [], 0
    seen = {}
    for k, (array, where, first) in enumerate(queries):
        for f, i in where.items():
            for b in range(array.shape[-1] // lanes):
                places.append((k, f, i, b, first + b))
                seen[first + b] = True
    slabs = len(seen)

    def kernel(end_ref, state_ref, gain_ref, *rest):
        prior_refs, q_refs = rest[:n_prior], rest[n_prior : n_prior + n_q]
        outs = rest[n_prior + n_q :]
        prior = jnp.zeros((group, HD), F32)
        for p in prior_refs:
            prior = prior + p[...].astype(F32)
        block = []
        for f in range(frames):
            total = prior
            for g in range(frames):
                seen_by = (end_ref[g] <= end_ref[f]).astype(F32)
                total = total + seen_by * state_ref[g]
            block.append(total.astype(BF16))
        for k, f, i, b, slab in places:
            for h in range(heads):
                rows = slice(h * HD, (h + 1) * HD)
                a = dot(block[f][rows], q_refs[k][i, rows, b * lanes : (b + 1) * lanes])
                mean = jnp.mean(a * a, axis=0, keepdims=True)
                outs[slab][f, rows, :] = (a * lax.rsqrt(mean + EPS) * gain_ref[rows]).astype(BF16)

    return pl.pallas_call(
        kernel,
        in_specs=[pl.BlockSpec(memory_space=pltpu.SMEM)]
        + [pl.BlockSpec(memory_space=pltpu.VMEM)] * (2 + n_prior + n_q),
        out_specs=[pl.BlockSpec(memory_space=pltpu.VMEM)] * slabs,
        out_shape=[jax.ShapeDtypeStruct((frames, group, lanes), BF16)] * slabs,
        compiler_params=params(),
        cost_estimate=cost(2 * group * HD * frames * slabs * lanes, 4 * group * frames * slabs * lanes),
        name="attend",
    )(end, states, head_gain, *priors, *[a for a, _, _ in queries])


def turn(here, own, other, blocks, cuts):
    group, width = own.shape
    rows = width // blocks
    sizes = [b - a for a, b in zip(cuts[:-1], cuts[1:])]

    def kernel(here_ref, own_ref, other_ref, whole_ref, *pieces):
        for first in range(2):

            @pl.when(here_ref[0] == first)
            def _():
                for k, ref in enumerate((own_ref, other_ref)):
                    at = (k ^ first) * group
                    whole_ref[:, at : at + group] = ref[...].T

        for a, piece in zip(cuts, pieces):
            start = pl.multiple_of(here_ref[1] * rows + a, 16)
            piece[...] = whole_ref[pl.ds(start, piece.shape[0]), :]

    return pl.pallas_call(
        kernel,
        in_specs=[pl.BlockSpec(memory_space=pltpu.SMEM)] + [VMEM] * 2,
        out_specs=[VMEM] * (1 + len(sizes)),
        out_shape=[jax.ShapeDtypeStruct((width, 2 * group), BF16)]
        + [jax.ShapeDtypeStruct((n, 2 * group), BF16) for n in sizes],
        compiler_params=params(),
        cost_estimate=cost(0, 16 * group * width),
        name="turn",
    )(here, own, other)


def pack(both, here_ref, mine, other):
    frames, group, lanes = mine.shape
    for f in range(frames):
        cols = slice(f * lanes, (f + 1) * lanes)
        for ref, at in ((mine, here_ref[0]), (other, 1 - here_ref[0])):
            both[pl.ds(pl.multiple_of(at * group, 16), group), cols] = ref[f]


def mix(here, weights, mine, other):
    frames, group, lanes = mine.shape
    width = weights.shape[0]

    def kernel(here_ref, w_ref, mine_ref, other_ref, out, both):
        pack(both, here_ref, mine_ref, other_ref)
        total = dot(w_ref[...], both[...])
        for f in range(frames):
            out[f] = total[:, f * lanes : (f + 1) * lanes]

    return pl.pallas_call(
        kernel,
        in_specs=[pl.BlockSpec(memory_space=pltpu.SMEM)] + [VMEM] * 3,
        out_specs=VMEM,
        out_shape=jax.ShapeDtypeStruct((frames, width, lanes), F32),
        scratch_shapes=[pltpu.VMEM((2 * group, frames * lanes), BF16)],
        compiler_params=params(),
        cost_estimate=cost(4 * width * group * frames * lanes, 4 * width * group),
        name="mix",
    )(here, weights, mine, other)


def finish(here, order, own, chips):
    frames, width, lanes = own.shape
    blocks = len(order)
    rows = width // blocks
    counts = [[len(p) for p in pieces] for pieces, _, _ in chips]
    group = chips[0][1].shape[1]
    given = []
    for pieces, mine, other in chips:
        given += [mine, other] + [v for p in pieces for v in p]

    def kernel(order_ref, here_ref, own_ref, *refs):
        refs, out, both, w = refs[: len(given)], refs[-3], refs[-2], refs[-1]
        step = pl.program_id(0)

        @pl.when(step == 0)
        def _():
            at = 0
            for k, count in enumerate(counts):
                pack(both.at[k], here_ref, refs[at], refs[at + 1])
                at += 2 + sum(count)

        at = 0
        for k, count in enumerate(counts):
            at += 2
            for r, n in enumerate(count):

                @pl.when(step == r)
                def _(k=k, first=at, n=n):
                    row = 0
                    for ref in refs[first : first + n]:
                        w[k, row : row + ref.shape[0], :] = ref[...]
                        row += ref.shape[0]

                at += n
        total = None
        for k in range(len(counts)):
            term = dot(w[k], both[k])
            total = term if total is None else total + term
        for f in range(frames):
            out[f] = (own_ref[f] + total[:, f * lanes : (f + 1) * lanes]).astype(BF16)

    block = pl.BlockSpec((frames, rows, lanes), lambda g, order_ref, here_ref: (0, order_ref[g], 0))
    return pl.pallas_call(
        kernel,
        grid_spec=pltpu.PrefetchScalarGridSpec(
            num_scalar_prefetch=2,
            grid=(blocks,),
            in_specs=[block] + [VMEM] * len(given),
            out_specs=block,
            scratch_shapes=[
                pltpu.VMEM((len(chips), 2 * group, frames * lanes), BF16),
                pltpu.VMEM((len(chips), rows, 2 * group), BF16),
            ],
        ),
        out_shape=jax.ShapeDtypeStruct(own.shape, BF16),
        compiler_params=params(),
        cost_estimate=cost(4 * len(chips) * width * group * frames * lanes, 4 * len(chips) * width * group),
        name="finish",
    )(jnp.stack(order), here, own, *given)


CUTS = (0.0, 0.34, 0.68, 1.0)


def per_device(n_grp, n_row, n_frm, hidden_in, norm_gain, qkv_weight, head_gain, output_matrix, block_end):
    def swap(v, k, axis="row"):
        size = {"row": n_row, "grp": n_grp}[axis]
        return lax.ppermute(v, axis, [(i, i ^ k) for i in range(size)])

    def shift(v, s):
        return lax.ppermute(v, "frm", [(i, i + s) for i in range(n_frm - s)])

    lanes, frames, features = hidden_in.shape
    tokens = jnp.transpose(hidden_in, (1, 2, 0))
    weights = jnp.transpose(qkv_weight, (1, 2, 0)).reshape(-1, features)
    gain = norm_gain.reshape(features, 1)
    out_gain = head_gain.reshape(-1, 1)

    pairs = n_row // 2
    crossed = {}
    for f in range(frames):
        for k in range(1, pairs):
            crossed[k, f] = swap(tokens[f], 2 * k)
    sibling = swap(tokens, 1)
    passed = {key: swap(v, 1) for key, v in crossed.items()}

    where = [[(0, f), (1, f)] for f in range(frames)]
    states, near_q = project([tokens, sibling], where, gain, weights, None, frames)
    width = output_matrix.shape[1]
    core = lax.axis_index("row") % 2
    grp = lax.axis_index("grp")
    blocks = 2 * n_grp
    here = jnp.stack([core, 2 * grp + core])
    cuts = [int(c * (width // blocks)) // 16 * 16 for c in CUTS]
    near_rows = swap(output_matrix, 1)
    turned, *pieces = turn(here, output_matrix, near_rows, blocks, cuts)
    states, turned = lax.optimization_barrier((states, turned))

    order, chips = [], []
    for g in range(n_grp):
        for c in range(2):
            order.append(2 * (grp ^ g) + (core ^ c))
    for k in range(1, pairs):
        held = {}
        for j, piece in enumerate(pieces):
            held[0, 0, j] = swap(piece, 2 * k)
            for g in range(1, n_grp):
                held[g, 0, j] = swap(held[0, 0, j], g, "grp")
            for g in range(n_grp):
                held[g, 1, j] = swap(held[g, 0, j], 1)
        chips.append([[held[g, c, j] for j in range(len(pieces))] for g in range(n_grp) for c in range(2)])
    queries = []
    for f in range(frames):
        for k in range(1, pairs):
            last = f == frames - 1 and k == pairs - 1
            blocks = [crossed[k, f], passed[k, f]]
            out = project(blocks, [[(0, None), (1, None)]], gain, weights, states, frames, f, last)
            states = out[0]
            if last:
                own_sum, normed = out[1:]
            else:
                queries.append((out[1], {f: 0}, 2 * k))
    if n_frm <= 4:
        priors = [shift(own_sum, s) for s in range(1, n_frm)]
    else:
        total, s = shift(own_sum.astype(F32), 1), 1
        while s < n_frm:
            total, s = total + shift(total, s), 2 * s
        priors = [total]
    queries.append((query(normed, weights), {frames - 1: 0}, n_row - 2))
    queries.append((near_q, {f: f for f in range(frames)}, 0))
    heads_out = attend(block_end, states, priors, out_gain, queries, lanes)

    across = []
    for k in range(1, pairs):
        across.append((swap(heads_out[2 * k], 2 * k), swap(heads_out[2 * k + 1], 2 * k + 1)))
    own = mix(here, turned, heads_out[0], swap(heads_out[1], 1))
    chips = [(held, *pair) for held, pair in zip(chips, across)]
    out = finish(here, order, own, chips)
    return jnp.transpose(out, (2, 0, 1))


def solution(mesh):
    placed = (
        P("row", ("grp", "frm"), None),
        P(),
        P(None, None, "row"),
        P("row"),
        P("row", None),
        P(("grp", "frm")),
    )

    def body(*args):
        return per_device(mesh.shape["grp"], mesh.shape["row"], mesh.shape["frm"], *args)

    return jax.shard_map(
        body, mesh=mesh, in_specs=placed, out_specs=P("row", ("grp", "frm"), None), check_vma=False
    )
```

```python
import jax
import jax.numpy as jnp
from jax import lax
from jax.experimental import pallas as pl
from jax.experimental.pallas import tpu as pltpu
from jax.sharding import PartitionSpec as P


HD = 112
EPS = 1e-06
F32 = jnp.float32
BF16 = jnp.bfloat16


def cost(flops, nbytes):
    return pl.CostEstimate(flops=int(flops), bytes_accessed=int(nbytes), transcendentals=0)


def params(mib=24):
    return pltpu.CompilerParams(vmem_limit_bytes=mib << 20)


def dot(a, b):
    return jnp.dot(a, b, preferred_element_type=F32)


def dot_nt(a, b):
    return lax.dot_general(a, b, (((1,), (1,)), ((), ())), preferred_element_type=F32)


VMEM = pl.BlockSpec(memory_space=pltpu.VMEM)


def scaled(x_ref, gain_ref):
    x = x_ref[...].astype(F32)
    mean = jnp.mean(x * x, axis=0, keepdims=True)
    return (x * lax.rsqrt(mean + EPS) * gain_ref[...]).astype(BF16)


def project(blocks, where, gain, weights, states=None, frames=1, first=0, last=False):
    n = len(blocks)
    here, per_frame = len(where), len(where[0])
    features, lanes = blocks[0].shape[-2:]
    group = weights.shape[0] // 3
    heads = group // HD
    width = per_frame * lanes
    total = here * width
    begin = group if last else 0

    def kernel(*refs):
        x_refs, rest = refs[:n], refs[n:]
        gain_ref, w_ref, rest = rest[0], rest[1], rest[2:]
        if states is not None:
            old, rest = rest[0], rest[1:]
        state, second, normed, part = rest[0], rest[1], rest[-2], rest[-1]
        if last:
            normed = rest[2]
        for f in range(here):
            for b, (k, i) in enumerate(where[f]):
                block = x_refs[k] if i is None else x_refs[k].at[i]
                at = f * width + b * lanes
                normed[:, at : at + lanes] = scaled(block, gain_ref)
        part[...] = jnp.dot(w_ref[begin:, :], normed[...], preferred_element_type=F32).astype(BF16)
        keys, values = group - begin, 2 * group - begin
        for f in range(here):
            cols = slice(f * width, (f + 1) * width)
            for h in range(heads):
                k = jnp.maximum(part[keys + h * HD : keys + (h + 1) * HD, cols], 0.0)
                v = part[values + h * HD : values + (h + 1) * HD, cols]
                rows = slice(h * HD, (h + 1) * HD)
                add = dot_nt(v, k)
                state[first + f, rows, :] = add if states is None else old[first + f, rows, :] + add
        if states is not None:
            for f in range(frames):
                if not first <= f < first + here:
                    state[f] = old[f]
        if last:
            own = state[0]
            for f in range(1, frames):
                own = own + state[f]
            second[...] = own.astype(BF16)
        else:
            for f in range(here):
                second[f] = jnp.maximum(part[:group, f * width : (f + 1) * width], 0.0)

    out_shape = [jax.ShapeDtypeStruct((frames, group, HD), F32)]
    scratch = [pltpu.VMEM((3 * group - begin, total), BF16)]
    if last:
        out_shape.append(jax.ShapeDtypeStruct((group, HD), BF16))
        out_shape.append(jax.ShapeDtypeStruct((features, total), BF16))
    else:
        out_shape.append(jax.ShapeDtypeStruct((here, group, width), BF16))
        scratch = [pltpu.VMEM((features, total), BF16)] + scratch
    given = [*blocks, gain, weights] + ([] if states is None else [states])
    return pl.pallas_call(
        kernel,
        in_specs=[VMEM] * len(given),
        out_specs=[VMEM] * len(out_shape),
        out_shape=out_shape,
        scratch_shapes=scratch,
        compiler_params=params(),
        cost_estimate=cost(2 * (3 * group - begin) * features * total, 2 * features * total),
        name="project",
    )(*given)


def query(normed, weights):
    features, total = normed.shape
    group = weights.shape[0] // 3

    def kernel(x_ref, w_ref, q_ref):
        q_ref[0] = jnp.maximum(dot(w_ref[:group, :], x_ref[...]), 0.0).astype(BF16)

    return pl.pallas_call(
        kernel,
        in_specs=[VMEM] * 2,
        out_specs=VMEM,
        out_shape=jax.ShapeDtypeStruct((1, group, total), BF16),
        compiler_params=params(),
        cost_estimate=cost(2 * group * features * total, 2 * features * total),
        name="query",
    )(normed, weights)


def attend(end, states, priors, head_gain, queries, lanes):
    frames, group, _ = states.shape
    heads = group // HD
    n_prior, n_q = len(priors), len(queries)
    places, slabs = [], 0
    seen = {}
    for k, (array, where, first) in enumerate(queries):
        for f, i in where.items():
            for b in range(array.shape[-1] // lanes):
                places.append((k, f, i, b, first + b))
                seen[first + b] = True
    slabs = len(seen)

    def kernel(end_ref, state_ref, gain_ref, *rest):
        prior_refs, q_refs = rest[:n_prior], rest[n_prior : n_prior + n_q]
        outs = rest[n_prior + n_q :]
        prior = jnp.zeros((group, HD), F32)
        for p in prior_refs:
            prior = prior + p[...].astype(F32)
        block = []
        for f in range(frames):
            total = prior
            for g in range(frames):
                seen_by = (end_ref[g] <= end_ref[f]).astype(F32)
                total = total + seen_by * state_ref[g]
            block.append(total.astype(BF16))
        for k, f, i, b, slab in places:
            for h in range(heads):
                rows = slice(h * HD, (h + 1) * HD)
                a = dot(block[f][rows], q_refs[k][i, rows, b * lanes : (b + 1) * lanes])
                mean = jnp.mean(a * a, axis=0, keepdims=True)
                outs[slab][f, rows, :] = (a * lax.rsqrt(mean + EPS) * gain_ref[rows]).astype(BF16)

    return pl.pallas_call(
        kernel,
        in_specs=[pl.BlockSpec(memory_space=pltpu.SMEM)]
        + [pl.BlockSpec(memory_space=pltpu.VMEM)] * (2 + n_prior + n_q),
        out_specs=[pl.BlockSpec(memory_space=pltpu.VMEM)] * slabs,
        out_shape=[jax.ShapeDtypeStruct((frames, group, lanes), BF16)] * slabs,
        compiler_params=params(),
        cost_estimate=cost(2 * group * HD * frames * slabs * lanes, 4 * group * frames * slabs * lanes),
        name="attend",
    )(end, states, head_gain, *priors, *[a for a, _, _ in queries])


def cut(source, start, sizes, aligned):
    width = source.shape[-1]

    def kernel(start_ref, src, *rest):
        outs, sem = rest[: len(sizes)], rest[-1]
        copies, at = [], 0
        for k, (out, n) in enumerate(zip(outs, sizes)):
            if source.ndim == 3:
                view = src.at[start]
            else:
                view = src.at[pl.ds(pl.multiple_of(start_ref[0] + at, aligned), n), :]
            copies.append(pltpu.make_async_copy(view, out, sem.at[k]))
            copies[-1].start()
            at += n
        for c in copies:
            c.wait()

    where = jnp.zeros((1,), jnp.int32) if source.ndim == 3 else start.reshape(1)
    return pl.pallas_call(
        kernel,
        in_specs=[pl.BlockSpec(memory_space=pltpu.SMEM), pl.BlockSpec(memory_space=pl.ANY)],
        out_specs=[VMEM] * len(sizes),
        out_shape=[jax.ShapeDtypeStruct((n, width), source.dtype) for n in sizes],
        scratch_shapes=[pltpu.SemaphoreType.DMA((len(sizes),))],
        compiler_params=params(),
        cost_estimate=cost(0, 4 * sum(sizes) * width),
        name="cut",
    )(where, source)


def tokens_first(refs):
    frames = refs[0].shape[0]
    return [jnp.concatenate([r[f] for r in refs], axis=0).T for f in range(frames)]


def mix(rows, heads_out):
    frames, group, lanes = heads_out[0].shape
    width = rows[0].shape[1]
    n = len(rows)

    def kernel(*refs):
        out = refs[2 * n]
        total = None
        for w, x in zip(refs[:n], refs[n : 2 * n]):
            left = jnp.concatenate(tokens_first([x]), axis=0)
            term = dot(left, w[...])
            total = term if total is None else total + term
        out[...] = total

    return pl.pallas_call(
        kernel,
        in_specs=[VMEM] * (2 * n),
        out_specs=VMEM,
        out_shape=jax.ShapeDtypeStruct((frames * lanes, width), F32),
        compiler_params=params(),
        cost_estimate=cost(4 * width * group * frames * lanes, 4 * width * group),
        name="mix",
    )(*rows, *heads_out)


def finish(starts, own, chips, shape):
    frames, width, lanes = shape
    group = chips[0][0][0].shape[1]
    given, plan = [], []
    for heads_out, cores in chips:
        plan.append((len(given), []))
        given += heads_out
        for core, lists in enumerate(cores):
            for g, pieces in enumerate(lists):
                at = 0
                for p in pieces:
                    plan[-1][1].append((len(given), core, g, at))
                    given.append(p)
                    at += p.shape[0]
    n = len(given)
    step = 640 if width > 640 else width
    spans = [(a, min(a + step, width)) for a in range(0, width, step)]

    def kernel(start_ref, own_ref, *refs):
        out, w = refs[n], refs[n + 1]
        lefts = []
        for k, (first, pieces) in enumerate(plan):
            for i, core, g, at in pieces:
                row = pl.multiple_of(start_ref[g] + (core * group + at), 16)
                w[k, pl.ds(row, refs[i].shape[0]), :] = refs[i][...]
            lefts.append(jnp.concatenate(tokens_first(refs[first : first + 2]), axis=0))
        for a, b in spans:
            total = own_ref[:, a:b]
            for k, left in enumerate(lefts):
                total = total + dot(left, w[k, :, a:b])
            total = total.astype(BF16)
            for f in range(frames):
                out[f, a:b, :] = total[f * lanes : (f + 1) * lanes].T

    return pl.pallas_call(
        kernel,
        in_specs=[pl.BlockSpec(memory_space=pltpu.SMEM)] + [VMEM] * (1 + n),
        out_specs=VMEM,
        out_shape=jax.ShapeDtypeStruct(shape, BF16),
        scratch_shapes=[pltpu.VMEM((len(chips), 2 * group, width), BF16)],
        compiler_params=params(),
        cost_estimate=cost(4 * len(chips) * width * group * frames * lanes, 4 * len(chips) * width * group),
        name="finish",
    )(starts, own, *given)


PIECES = 3


def per_device(n_grp, n_row, n_frm, hidden_in, norm_gain, qkv_weight, head_gain, output_matrix, block_end):
    def swap(v, k, axis="row"):
        size = {"row": n_row, "grp": n_grp}[axis]
        return lax.ppermute(v, axis, [(i, i ^ k) for i in range(size)])

    def shift(v, s):
        return lax.ppermute(v, "frm", [(i, i + s) for i in range(n_frm - s)])

    lanes, frames, features = hidden_in.shape
    tokens = jnp.transpose(hidden_in, (1, 2, 0))
    weights = jnp.transpose(qkv_weight, (1, 2, 0)).reshape(-1, features)
    gain = norm_gain.reshape(features, 1)
    out_gain = head_gain.reshape(-1, 1)

    pairs = n_row // 2
    crossed = {}
    for f in range(frames):
        (frame,) = cut(tokens, f, [features], 1)
        for k in range(1, pairs):
            crossed[k, f] = swap(frame, 2 * k)
    sibling = swap(tokens, 1)
    passed = {key: swap(v, 1) for key, v in crossed.items()}

    where = [[(0, f), (1, f)] for f in range(frames)]
    states, near_q = project([tokens, sibling], where, gain, weights, None, frames)

    group, width = output_matrix.shape
    grp = lax.axis_index("grp")
    share = -(-group // (16 * n_grp)) * 16
    stride = (group - share) // max(n_grp - 1, 1)
    sizes = [share // 16 * (j + 1) // PIECES * 16 - share // 16 * j // PIECES * 16 for j in range(PIECES)]
    pieces = cut(output_matrix, grp * stride, sizes, 16)
    near_rows = swap(output_matrix, 1)
    starts = jnp.stack([(grp ^ g) * stride for g in range(n_grp)])
    far_rows = []
    for k in range(1, pairs):
        held = {}
        for j, piece in enumerate(pieces):
            held[0, 0, j] = swap(piece, 2 * k)
            for g in range(1, n_grp):
                held[0, g, j] = swap(held[0, 0, j], g, "grp")
            for g in range(n_grp):
                held[1, g, j] = swap(held[0, g, j], 1)
        far_rows.append([[[held[c, g, j] for j in range(PIECES)] for g in range(n_grp)] for c in range(2)])
    queries = []
    for f in range(frames):
        for k in range(1, pairs):
            last = f == frames - 1 and k == pairs - 1
            blocks = [crossed[k, f], passed[k, f]]
            out = project(blocks, [[(0, None), (1, None)]], gain, weights, states, frames, f, last)
            states = out[0]
            if last:
                own_sum, normed = out[1:]
            else:
                queries.append((out[1], {f: 0}, 2 * k))
    if n_frm <= 4:
        priors = [shift(own_sum, s) for s in range(1, n_frm)]
    else:
        total, s = shift(own_sum.astype(F32), 1), 1
        while s < n_frm:
            total, s = total + shift(total, s), 2 * s
        priors = [total]
    queries.append((query(normed, weights), {frames - 1: 0}, n_row - 2))
    queries.append((near_q, {f: f for f in range(frames)}, 0))
    heads_out = attend(block_end, states, priors, out_gain, queries, lanes)

    across = []
    for k in range(1, pairs):
        across.append((swap(heads_out[2 * k], 2 * k), swap(heads_out[2 * k + 1], 2 * k + 1)))
    own = mix([output_matrix, near_rows], [heads_out[0], swap(heads_out[1], 1)])
    out = finish(starts, own, list(zip(across, far_rows)), (frames, width, lanes))
    return jnp.transpose(out, (2, 0, 1))


def solution(mesh):
    placed = (
        P("row", ("grp", "frm"), None),
        P(),
        P(None, None, "row"),
        P("row"),
        P("row", None),
        P(("grp", "frm")),
    )

    def body(*args):
        return per_device(mesh.shape["grp"], mesh.shape["row"], mesh.shape["frm"], *args)

    return jax.shard_map(
        body, mesh=mesh, in_specs=placed, out_specs=P("row", ("grp", "frm"), None), check_vma=False
    )
```

```python
import jax
import jax.numpy as jnp
from jax import lax
from jax.experimental import pallas as pl
from jax.experimental.pallas import tpu as pltpu
from jax.sharding import PartitionSpec as P


HD = 112
EPS = 1e-06
F32 = jnp.float32
BF16 = jnp.bfloat16


def cost(flops, nbytes):
    return pl.CostEstimate(flops=int(flops), bytes_accessed=int(nbytes), transcendentals=0)


def params(mib=24):
    return pltpu.CompilerParams(vmem_limit_bytes=mib << 20)


def dot(a, b):
    return jnp.dot(a, b, preferred_element_type=F32)


def dot_nt(a, b):
    return lax.dot_general(a, b, (((1,), (1,)), ((), ())), preferred_element_type=F32)


VMEM = pl.BlockSpec(memory_space=pltpu.VMEM)


def scaled(x_ref, gain_ref):
    x = x_ref[...].astype(F32)
    mean = jnp.mean(x * x, axis=0, keepdims=True)
    return (x * lax.rsqrt(mean + EPS) * gain_ref[...]).astype(BF16)


def project(blocks, where, gain, weights, states=None, frames=1, first=0, last=False):
    n = len(blocks)
    here, per_frame = len(where), len(where[0])
    features, lanes = blocks[0].shape[-2:]
    group = weights.shape[0] // 3
    heads = group // HD
    width = per_frame * lanes
    total = here * width
    begin = group if last else 0

    def kernel(*refs):
        x_refs, rest = refs[:n], refs[n:]
        gain_ref, w_ref, rest = rest[0], rest[1], rest[2:]
        if states is not None:
            old, rest = rest[0], rest[1:]
        state, second, normed, part = rest[0], rest[1], rest[-2], rest[-1]
        if last:
            normed = rest[2]
        for f in range(here):
            for b, (k, i) in enumerate(where[f]):
                block = x_refs[k] if i is None else x_refs[k].at[i]
                at = f * width + b * lanes
                normed[:, at : at + lanes] = scaled(block, gain_ref)
        part[...] = jnp.dot(w_ref[begin:, :], normed[...], preferred_element_type=F32).astype(BF16)
        keys, values = group - begin, 2 * group - begin
        for f in range(here):
            cols = slice(f * width, (f + 1) * width)
            for h in range(heads):
                k = jnp.maximum(part[keys + h * HD : keys + (h + 1) * HD, cols], 0.0)
                v = part[values + h * HD : values + (h + 1) * HD, cols]
                rows = slice(h * HD, (h + 1) * HD)
                add = dot_nt(v, k)
                state[first + f, rows, :] = add if states is None else old[first + f, rows, :] + add
        if states is not None:
            for f in range(frames):
                if not first <= f < first + here:
                    state[f] = old[f]
        if last:
            own = state[0]
            for f in range(1, frames):
                own = own + state[f]
            second[...] = own.astype(BF16)
        else:
            for f in range(here):
                second[f] = jnp.maximum(part[:group, f * width : (f + 1) * width], 0.0)

    out_shape = [jax.ShapeDtypeStruct((frames, group, HD), F32)]
    scratch = [pltpu.VMEM((3 * group - begin, total), BF16)]
    if last:
        out_shape.append(jax.ShapeDtypeStruct((group, HD), BF16))
        out_shape.append(jax.ShapeDtypeStruct((features, total), BF16))
    else:
        out_shape.append(jax.ShapeDtypeStruct((here, group, width), BF16))
        scratch = [pltpu.VMEM((features, total), BF16)] + scratch
    given = [*blocks, gain, weights] + ([] if states is None else [states])
    return pl.pallas_call(
        kernel,
        in_specs=[VMEM] * len(given),
        out_specs=[VMEM] * len(out_shape),
        out_shape=out_shape,
        scratch_shapes=scratch,
        compiler_params=params(),
        cost_estimate=cost(2 * (3 * group - begin) * features * total, 2 * features * total),
        name="project",
    )(*given)


def query(normed, weights, frames):
    features, total = normed.shape
    group = weights.shape[0] // 3
    width = total // frames

    def kernel(x_ref, w_ref, q_ref):
        q = jnp.maximum(dot(w_ref[:group, :], x_ref[...]), 0.0).astype(BF16)
        for f in range(frames):
            q_ref[f] = q[:, f * width : (f + 1) * width]

    return pl.pallas_call(
        kernel,
        in_specs=[VMEM] * 2,
        out_specs=VMEM,
        out_shape=jax.ShapeDtypeStruct((frames, group, width), BF16),
        compiler_params=params(),
        cost_estimate=cost(2 * group * features * total, 2 * features * total),
        name="query",
    )(normed, weights)


def attend(end, states, priors, head_gain, queries, lanes):
    frames, group, _ = states.shape
    heads = group // HD
    n_prior, n_q = len(priors), len(queries)
    places, slabs = [], 0
    seen = {}
    for k, (array, where, first) in enumerate(queries):
        for f, i in where.items():
            for b in range(array.shape[-1] // lanes):
                places.append((k, f, i, b, first + b))
                seen[first + b] = True
    slabs = len(seen)

    def kernel(end_ref, state_ref, gain_ref, *rest):
        prior_refs, q_refs = rest[:n_prior], rest[n_prior : n_prior + n_q]
        outs = rest[n_prior + n_q :]
        prior = jnp.zeros((group, HD), F32)
        for p in prior_refs:
            prior = prior + p[...].astype(F32)
        block = []
        for f in range(frames):
            total = prior
            for g in range(frames):
                seen_by = (end_ref[g] <= end_ref[f]).astype(F32)
                total = total + seen_by * state_ref[g]
            block.append(total.astype(BF16))
        for k, f, i, b, slab in places:
            for h in range(heads):
                rows = slice(h * HD, (h + 1) * HD)
                a = dot(block[f][rows], q_refs[k][i, rows, b * lanes : (b + 1) * lanes])
                mean = jnp.mean(a * a, axis=0, keepdims=True)
                outs[slab][f, rows, :] = (a * lax.rsqrt(mean + EPS) * gain_ref[rows]).astype(BF16)

    return pl.pallas_call(
        kernel,
        in_specs=[pl.BlockSpec(memory_space=pltpu.SMEM)]
        + [pl.BlockSpec(memory_space=pltpu.VMEM)] * (2 + n_prior + n_q),
        out_specs=[pl.BlockSpec(memory_space=pltpu.VMEM)] * slabs,
        out_shape=[jax.ShapeDtypeStruct((frames, group, lanes), BF16)] * slabs,
        compiler_params=params(),
        cost_estimate=cost(2 * group * HD * frames * slabs * lanes, 4 * group * frames * slabs * lanes),
        name="attend",
    )(end, states, head_gain, *priors, *[a for a, _, _ in queries])


def cut(source, start, sizes, aligned):
    width = source.shape[-1]

    def kernel(start_ref, src, *rest):
        outs, sem = rest[: len(sizes)], rest[-1]
        copies, at = [], 0
        for k, (out, n) in enumerate(zip(outs, sizes)):
            view = src.at[pl.ds(pl.multiple_of(start_ref[0] + at, aligned), n), :]
            copies.append(pltpu.make_async_copy(view, out, sem.at[k]))
            copies[-1].start()
            at += n
        for c in copies:
            c.wait()

    return pl.pallas_call(
        kernel,
        in_specs=[pl.BlockSpec(memory_space=pltpu.SMEM), pl.BlockSpec(memory_space=pl.ANY)],
        out_specs=[VMEM] * len(sizes),
        out_shape=[jax.ShapeDtypeStruct((n, width), source.dtype) for n in sizes],
        scratch_shapes=[pltpu.SemaphoreType.DMA((len(sizes),))],
        compiler_params=params(),
        cost_estimate=cost(0, 4 * sum(sizes) * width),
        name="cut",
    )(start.reshape(1), source)


def tokens_first(ref):
    return jnp.concatenate([ref[f].T for f in range(ref.shape[0])], axis=0)


def mix(rows, heads_out):
    frames, group, lanes = heads_out[0].shape
    width = rows[0].shape[1]
    n = len(rows)

    def kernel(*refs):
        out = refs[2 * n]
        total = None
        for w, x in zip(refs[:n], refs[n : 2 * n]):
            term = dot(tokens_first(x), w[...])
            total = term if total is None else total + term
        out[...] = total

    return pl.pallas_call(
        kernel,
        in_specs=[VMEM] * (2 * n),
        out_specs=VMEM,
        out_shape=jax.ShapeDtypeStruct((frames * lanes, width), F32),
        compiler_params=params(),
        cost_estimate=cost(4 * width * group * frames * lanes, 4 * width * group),
        name="mix",
    )(*rows, *heads_out)


def add_heads(starts, total, heads_out, lists, last):
    frames, group, lanes = heads_out.shape
    width = total.shape[1]
    given, plan = [], []
    for g, pieces in enumerate(lists):
        at = 0
        for p in pieces:
            plan.append((g, at))
            given.append(p)
            at += p.shape[0]
    n = len(given)
    step = 640 if width > 640 else width
    spans = [(a, min(a + step, width)) for a in range(0, width, step)]

    def kernel(start_ref, total_ref, heads_ref, *refs):
        out, w = refs[n], refs[n + 1]
        for ref, (g, at) in zip(refs[:n], plan):
            row = pl.multiple_of(start_ref[g] + at, 16)
            w[pl.ds(row, ref.shape[0]), :] = ref[...]
        left = tokens_first(heads_ref)
        for a, b in spans:
            now = total_ref[:, a:b] + dot(left, w[:, a:b])
            if not last:
                out[:, a:b] = now
                continue
            now = now.astype(BF16)
            for f in range(frames):
                out[f, a:b, :] = now[f * lanes : (f + 1) * lanes].T

    shape = (frames, width, lanes) if last else total.shape
    return pl.pallas_call(
        kernel,
        in_specs=[pl.BlockSpec(memory_space=pltpu.SMEM)] + [VMEM] * (2 + n),
        out_specs=VMEM,
        out_shape=jax.ShapeDtypeStruct(shape, BF16 if last else F32),
        scratch_shapes=[pltpu.VMEM((group, width), BF16)],
        compiler_params=params(),
        cost_estimate=cost(2 * width * group * frames * lanes, 2 * width * group),
        name="add_heads",
    )(starts, total, heads_out, *given)


PIECES = 3


def per_device(n_grp, n_row, n_frm, hidden_in, norm_gain, qkv_weight, head_gain, output_matrix, block_end):
    def swap(v, k, axis="row"):
        size = {"row": n_row, "grp": n_grp}[axis]
        return lax.ppermute(v, axis, [(i, i ^ k) for i in range(size)])

    def shift(v, s):
        return lax.ppermute(v, "frm", [(i, i + s) for i in range(n_frm - s)])

    lanes, frames, features = hidden_in.shape
    tokens = jnp.transpose(hidden_in, (1, 2, 0))
    weights = jnp.transpose(qkv_weight, (1, 2, 0)).reshape(-1, features)
    gain = norm_gain.reshape(features, 1)
    out_gain = head_gain.reshape(-1, 1)

    pairs = n_row // 2
    crossed = {k: swap(tokens, 2 * k) for k in range(1, pairs)}
    sibling = swap(tokens, 1)
    passed = {k: swap(v, 1) for k, v in crossed.items()}

    where = [[(0, f), (1, f)] for f in range(frames)]
    states, near_q = project([tokens, sibling], where, gain, weights, None, frames)

    group, _ = output_matrix.shape
    grp = lax.axis_index("grp")
    share = -(-group // (16 * n_grp)) * 16
    stride = (group - share) // max(n_grp - 1, 1)
    sizes = [share // 16 * (j + 1) // PIECES * 16 - share // 16 * j // PIECES * 16 for j in range(PIECES)]
    pieces = cut(output_matrix, grp * stride, sizes, 16)
    near_rows = swap(output_matrix, 1)
    starts = jnp.stack([(grp ^ g) * stride for g in range(n_grp)])
    far_rows = []
    for k in range(1, pairs):
        held = {}
        for j, piece in enumerate(pieces):
            held[0, 0, j] = swap(piece, 2 * k)
            for g in range(1, n_grp):
                held[0, g, j] = swap(held[0, 0, j], g, "grp")
            for g in range(n_grp):
                held[1, g, j] = swap(held[0, g, j], 1)
        far_rows.append([[[held[c, g, j] for j in range(PIECES)] for g in range(n_grp)] for c in range(2)])
    queries = [(near_q, {f: f for f in range(frames)}, 0)]
    for k in range(1, pairs):
        for c, block in enumerate((crossed[k], passed[k])):
            last = c == 1 and k == pairs - 1
            out = project([block], [[(0, f)] for f in range(frames)], gain, weights, states, frames, 0, last)
            states = out[0]
            if last:
                own_sum, normed = out[1:]
            else:
                queries.append((out[1], {f: f for f in range(frames)}, 2 * k + c))
    if n_frm <= 4:
        priors = [shift(own_sum, s) for s in range(1, n_frm)]
    else:
        total, s = shift(own_sum.astype(F32), 1), 1
        while s < n_frm:
            total, s = total + shift(total, s), 2 * s
        priors = [total]
    late = query(normed, weights, frames)
    queries.append((late, {f: f for f in range(frames)}, n_row - 1))
    heads_out = attend(block_end, states, priors, out_gain, queries, lanes)

    across = []
    for k in range(1, pairs):
        across.append((swap(heads_out[2 * k], 2 * k), swap(heads_out[2 * k + 1], 2 * k + 1)))
    own = mix([output_matrix, near_rows], [heads_out[0], swap(heads_out[1], 1)])
    total, left = own, 2 * (pairs - 1)
    for heads, rows in zip(across, far_rows):
        for c in range(2):
            left -= 1
            total = add_heads(starts, total, heads[c], rows[c], left == 0)
    return jnp.transpose(total, (2, 0, 1))


def solution(mesh):
    placed = (
        P("row", ("grp", "frm"), None),
        P(),
        P(None, None, "row"),
        P("row"),
        P("row", None),
        P(("grp", "frm")),
    )

    def body(*args):
        return per_device(mesh.shape["grp"], mesh.shape["row"], mesh.shape["frm"], *args)

    return jax.shard_map(
        body, mesh=mesh, in_specs=placed, out_specs=P("row", ("grp", "frm"), None), check_vma=False
    )
```

```python
import jax
import jax.numpy as jnp
from jax import lax
from jax.experimental import pallas as pl
from jax.experimental.pallas import tpu as pltpu
from jax.sharding import PartitionSpec as P


HD = 112
EPS = 1e-06
F32 = jnp.float32
BF16 = jnp.bfloat16


def cost(flops, nbytes):
    return pl.CostEstimate(flops=int(flops), bytes_accessed=int(nbytes), transcendentals=0)


def params(mib=24):
    return pltpu.CompilerParams(vmem_limit_bytes=mib << 20)


def dot(a, b):
    return jnp.dot(a, b, preferred_element_type=F32)


def dot_nt(a, b):
    return lax.dot_general(a, b, (((1,), (1,)), ((), ())), preferred_element_type=F32)


VMEM = pl.BlockSpec(memory_space=pltpu.VMEM)


def scaled(x_ref, gain_ref):
    x = x_ref[...].astype(F32)
    mean = jnp.mean(x * x, axis=0, keepdims=True)
    return (x * lax.rsqrt(mean + EPS) * gain_ref[...]).astype(BF16)


def project(blocks, where, gain, weights, states=None, frames=1, first=0, last=False):
    n = len(blocks)
    here, per_frame = len(where), len(where[0])
    features, lanes = blocks[0].shape[-2:]
    group = weights.shape[0] // 3
    heads = group // HD
    width = per_frame * lanes
    total = here * width
    begin = group if last else 0

    def kernel(*refs):
        x_refs, rest = refs[:n], refs[n:]
        gain_ref, w_ref, rest = rest[0], rest[1], rest[2:]
        if states is not None:
            old, rest = rest[0], rest[1:]
        state, second, normed, part = rest[0], rest[1], rest[-2], rest[-1]
        if last:
            normed = rest[2]
        for f in range(here):
            for b, (k, i) in enumerate(where[f]):
                block = x_refs[k] if i is None else x_refs[k].at[i]
                at = f * width + b * lanes
                normed[:, at : at + lanes] = scaled(block, gain_ref)
        part[...] = jnp.dot(w_ref[begin:, :], normed[...], preferred_element_type=F32).astype(BF16)
        keys, values = group - begin, 2 * group - begin
        for f in range(here):
            cols = slice(f * width, (f + 1) * width)
            for h in range(heads):
                k = jnp.maximum(part[keys + h * HD : keys + (h + 1) * HD, cols], 0.0)
                v = part[values + h * HD : values + (h + 1) * HD, cols]
                rows = slice(h * HD, (h + 1) * HD)
                add = dot_nt(v, k)
                state[first + f, rows, :] = add if states is None else old[first + f, rows, :] + add
        if states is not None:
            for f in range(frames):
                if not first <= f < first + here:
                    state[f] = old[f]
        if last:
            own = state[0]
            for f in range(1, frames):
                own = own + state[f]
            second[...] = own.astype(BF16)
        else:
            for f in range(here):
                second[f] = jnp.maximum(part[:group, f * width : (f + 1) * width], 0.0)

    out_shape = [jax.ShapeDtypeStruct((frames, group, HD), F32)]
    scratch = [pltpu.VMEM((3 * group - begin, total), BF16)]
    if last:
        out_shape.append(jax.ShapeDtypeStruct((group, HD), BF16))
        out_shape.append(jax.ShapeDtypeStruct((features, total), BF16))
    else:
        out_shape.append(jax.ShapeDtypeStruct((here, group, width), BF16))
        scratch = [pltpu.VMEM((features, total), BF16)] + scratch
    given = [*blocks, gain, weights] + ([] if states is None else [states])
    return pl.pallas_call(
        kernel,
        in_specs=[VMEM] * len(given),
        out_specs=[VMEM] * len(out_shape),
        out_shape=out_shape,
        scratch_shapes=scratch,
        compiler_params=params(),
        cost_estimate=cost(2 * (3 * group - begin) * features * total, 2 * features * total),
        name="project",
    )(*given)


def query(normed, weights, frames):
    features, total = normed.shape
    group = weights.shape[0] // 3
    width = total // frames

    def kernel(x_ref, w_ref, q_ref):
        q = jnp.maximum(dot(w_ref[:group, :], x_ref[...]), 0.0).astype(BF16)
        for f in range(frames):
            q_ref[f] = q[:, f * width : (f + 1) * width]

    return pl.pallas_call(
        kernel,
        in_specs=[VMEM] * 2,
        out_specs=VMEM,
        out_shape=jax.ShapeDtypeStruct((frames, group, width), BF16),
        compiler_params=params(),
        cost_estimate=cost(2 * group * features * total, 2 * features * total),
        name="query",
    )(normed, weights)


def attend(end, states, priors, head_gain, queries, lanes):
    frames, group, _ = states.shape
    heads = group // HD
    n_prior, n_q = len(priors), len(queries)
    places, slabs = [], 0
    seen = {}
    for k, (array, where, first) in enumerate(queries):
        for f, i in where.items():
            for b in range(array.shape[-1] // lanes):
                places.append((k, f, i, b, first + b))
                seen[first + b] = True
    slabs = len(seen)

    def kernel(end_ref, state_ref, gain_ref, *rest):
        prior_refs, q_refs = rest[:n_prior], rest[n_prior : n_prior + n_q]
        outs = rest[n_prior + n_q :]
        prior = jnp.zeros((group, HD), F32)
        for p in prior_refs:
            prior = prior + p[...].astype(F32)
        block = []
        for f in range(frames):
            total = prior
            for g in range(frames):
                seen_by = (end_ref[g] <= end_ref[f]).astype(F32)
                total = total + seen_by * state_ref[g]
            block.append(total.astype(BF16))
        for k, f, i, b, slab in places:
            for h in range(heads):
                rows = slice(h * HD, (h + 1) * HD)
                a = dot(block[f][rows], q_refs[k][i, rows, b * lanes : (b + 1) * lanes])
                mean = jnp.mean(a * a, axis=0, keepdims=True)
                outs[slab][f, rows, :] = (a * lax.rsqrt(mean + EPS) * gain_ref[rows]).astype(BF16)

    return pl.pallas_call(
        kernel,
        in_specs=[pl.BlockSpec(memory_space=pltpu.SMEM)]
        + [pl.BlockSpec(memory_space=pltpu.VMEM)] * (2 + n_prior + n_q),
        out_specs=[pl.BlockSpec(memory_space=pltpu.VMEM)] * slabs,
        out_shape=[jax.ShapeDtypeStruct((frames, group, lanes), BF16)] * slabs,
        compiler_params=params(),
        cost_estimate=cost(2 * group * HD * frames * slabs * lanes, 4 * group * frames * slabs * lanes),
        name="attend",
    )(end, states, head_gain, *priors, *[a for a, _, _ in queries])


def cut(source, starts, sizes):
    width = source.shape[-1]

    def kernel(start_ref, src, *rest):
        outs, sem = rest[: len(sizes)], rest[-1]
        copies = []
        for k, (out, n) in enumerate(zip(outs, sizes)):
            view = src.at[pl.ds(pl.multiple_of(start_ref[k], 16), n), :]
            copies.append(pltpu.make_async_copy(view, out, sem.at[k]))
            copies[-1].start()
        for c in copies:
            c.wait()

    return pl.pallas_call(
        kernel,
        in_specs=[pl.BlockSpec(memory_space=pltpu.SMEM), pl.BlockSpec(memory_space=pl.ANY)],
        out_specs=[VMEM] * len(sizes),
        out_shape=[jax.ShapeDtypeStruct((n, width), source.dtype) for n in sizes],
        scratch_shapes=[pltpu.SemaphoreType.DMA((len(sizes),))],
        compiler_params=params(8),
        cost_estimate=cost(0, 4 * sum(sizes) * width),
        name="cut",
    )(starts, source)


def copy_pieces(start_ref, refs, plan, matrix, sem):
    copies = []
    for i, (ref, (k, at)) in enumerate(zip(refs, plan)):
        row = pl.multiple_of(start_ref[k] + at, 16)
        copies.append(pltpu.make_async_copy(ref, matrix.at[pl.ds(row, ref.shape[0]), :], sem.at[i]))
        copies[-1].start()
    return copies


def place(starts, matrix, pieces, shape):
    n = len(pieces)
    plan = [(k, at) for _, k, at in pieces]

    def kernel(start_ref, *refs):
        for c in copy_pieces(start_ref, refs[:n], plan, refs[-2], refs[-1]):
            c.wait()

    given = [p for p, _, _ in pieces] + ([] if matrix is None else [matrix])
    return pl.pallas_call(
        kernel,
        in_specs=[pl.BlockSpec(memory_space=pltpu.SMEM)]
        + [pl.BlockSpec(memory_space=pl.ANY)] * n
        + ([] if matrix is None else [VMEM]),
        out_specs=VMEM,
        out_shape=pltpu.VMEM(shape, BF16),
        scratch_shapes=[pltpu.SemaphoreType.DMA((n,))],
        input_output_aliases={} if matrix is None else {1 + n: 0},
        compiler_params=params(8),
        cost_estimate=cost(0, sum(4 * p.size for p, _, _ in pieces)),
        name="place",
    )(starts, *given)


def tokens_first(ref):
    return jnp.concatenate([ref[f].T for f in range(ref.shape[0])], axis=0)


def mix(rows, heads_out):
    frames, group, lanes = heads_out[0].shape
    width = rows[0].shape[1]
    n = len(rows)

    def kernel(*refs):
        out = refs[2 * n]
        total = None
        for w, x in zip(refs[:n], refs[n : 2 * n]):
            term = dot(tokens_first(x), w[...])
            total = term if total is None else total + term
        out[...] = total

    return pl.pallas_call(
        kernel,
        in_specs=[VMEM] * (2 * n),
        out_specs=VMEM,
        out_shape=jax.ShapeDtypeStruct((frames * lanes, width), F32),
        compiler_params=params(),
        cost_estimate=cost(4 * width * group * frames * lanes, 4 * width * group),
        name="mix",
    )(*rows, *heads_out)


def add_heads(starts, total, heads_out, matrix, pieces, last):
    frames, group, lanes = heads_out[0].shape
    width = total.shape[1]
    n = len(pieces)
    plan = [(k, at) for _, k, at in pieces]
    step = 640 if width > 640 else width
    spans = [(a, min(a + step, width)) for a in range(0, width, step)]

    def kernel(start_ref, total_ref, x_ref, y_ref, *refs):
        out, w, sem = refs[n + 1], refs[n + 2], refs[n + 3]
        copies = copy_pieces(start_ref, refs[:n], plan, w, sem)
        left = jnp.concatenate(
            [jnp.concatenate([x_ref[f], y_ref[f]], axis=0).T for f in range(frames)], axis=0
        )
        for c in copies:
            c.wait()
        for a, b in spans:
            now = total_ref[:, a:b] + dot(left, w[:, a:b])
            if not last:
                out[:, a:b] = now
                continue
            now = now.astype(BF16)
            for f in range(frames):
                out[f, a:b, :] = now[f * lanes : (f + 1) * lanes].T

    shape = (frames, width, lanes) if last else total.shape
    return pl.pallas_call(
        kernel,
        in_specs=[pl.BlockSpec(memory_space=pltpu.SMEM)]
        + [VMEM] * 3
        + [pl.BlockSpec(memory_space=pl.ANY)] * n
        + [VMEM],
        out_specs=[VMEM] * 2,
        out_shape=[jax.ShapeDtypeStruct(shape, BF16 if last else F32), pltpu.VMEM(matrix.shape, BF16)],
        scratch_shapes=[pltpu.SemaphoreType.DMA((n,))],
        input_output_aliases={4 + n: 1},
        compiler_params=params(),
        cost_estimate=cost(4 * width * group * frames * lanes, 4 * width * group),
        name="add_heads",
    )(starts, total, *heads_out, *[p for p, _, _ in pieces], matrix)[0]


def per_device(n_grp, n_row, n_frm, hidden_in, norm_gain, qkv_weight, head_gain, output_matrix, block_end):
    def swap(v, k, axis="row"):
        size = {"row": n_row, "grp": n_grp, "frm": n_frm}[axis]
        return lax.ppermute(v, axis, [(i, i ^ k) for i in range(size)])

    def shift(v, s):
        return lax.ppermute(v, "frm", [(i, i + s) for i in range(n_frm - s)])

    lanes, frames, features = hidden_in.shape
    tokens = jnp.transpose(hidden_in, (1, 2, 0))
    weights = jnp.transpose(qkv_weight, (1, 2, 0)).reshape(-1, features)
    gain = norm_gain.reshape(features, 1)
    out_gain = head_gain.reshape(-1, 1)

    pairs = n_row // 2
    crossed = {k: swap(tokens, 2 * k) for k in range(1, pairs)}
    sibling = swap(tokens, 1)
    passed = {k: swap(v, 1) for k, v in crossed.items()}

    where = [[(0, f), (1, f)] for f in range(frames)]
    states, near_q = project([tokens, sibling], where, gain, weights, None, frames)


    group, width = output_matrix.shape
    grp = lax.axis_index("grp")
    side = lax.axis_index("frm") % 2
    share = -(-group // (16 * n_grp)) * 16
    stride = (group - share) // max(n_grp - 1, 1)
    half = share // 96 * 16
    outer = (share - 2 * half) // 32 * 16
    rest = share - 2 * half - outer
    base = grp * stride
    pieces = cut(
        output_matrix, jnp.stack([base, base + outer + side * half, base + outer + 2 * half]), [outer, half, rest]
    )
    near_rows = swap(output_matrix, 1)
    starts, index = [], {}
    for c in range(2):
        for g in range(n_grp):
            first = c * group + (grp ^ g) * stride
            for z, offset in enumerate((0, side * half, (1 - side) * half)):
                index[c, g, z] = len(starts)
                starts.append(first + offset)
    starts = jnp.stack(starts)
    far_rows = []
    for k in range(1, pairs):
        early, middle, late = [], [], []
        for j, piece in enumerate(pieces):
            held = [(0, 0, swap(piece, 2 * k))]
            for g in range(1, n_grp):
                held.append((g, 0, swap(held[0][2], g, "grp")))
            if j == 1:
                held += [(g, 1, swap(v, 1, "frm")) for g, _, v in held]
            for g, z, v in held:
                at = (0, outer, outer + 2 * half)[j]
                zone = 0 if j != 1 else 1 + z
                where_to = early if j == 0 else late if g and (j == 2 or z) else middle
                where_to.append((v, index[0, g, zone], at))
                where_to.append((swap(v, 1), index[1, g, zone], at))
        far_rows.append((early, middle, late))
    queries = [(near_q, {f: f for f in range(frames)}, 0)]
    for k in range(1, pairs):
        for c, block in enumerate((crossed[k], passed[k])):
            last = c == 1 and k == pairs - 1
            out = project([block], [[(0, f)] for f in range(frames)], gain, weights, states, frames, 0, last)
            states = out[0]
            if last:
                own_sum, normed = out[1:]
            else:
                queries.append((out[1], {f: f for f in range(frames)}, 2 * k + c))
    if n_frm <= 4:
        priors = [shift(own_sum, s) for s in range(1, n_frm)]
    else:
        total, s = shift(own_sum.astype(F32), 1), 1
        while s < n_frm:
            total, s = total + shift(total, s), 2 * s
        priors = [total]
    late = query(normed, weights, frames)
    queries.append((late, {f: f for f in range(frames)}, n_row - 1))
    heads_out = attend(block_end, states, priors, out_gain, queries, lanes)

    across = []
    for k in range(1, pairs):
        across.append((swap(heads_out[2 * k], 2 * k), swap(heads_out[2 * k + 1], 2 * k + 1)))
    own = mix([output_matrix, near_rows], [heads_out[0], swap(heads_out[1], 1)])
    total = own
    for k, (heads, (early, middle, late)) in enumerate(zip(across, far_rows)):
        shape = (2 * group, width)
        matrix = place(starts, None, early, shape)
        matrix = place(starts, matrix, middle, shape)
        total = add_heads(starts, total, heads, matrix, late, k == pairs - 2)
    return jnp.transpose(total, (2, 0, 1))


def solution(mesh):
    placed = (
        P("row", ("grp", "frm"), None),
        P(),
        P(None, None, "row"),
        P("row"),
        P("row", None),
        P(("grp", "frm")),
    )

    def body(*args):
        return per_device(mesh.shape["grp"], mesh.shape["row"], mesh.shape["frm"], *args)

    return jax.shard_map(
        body, mesh=mesh, in_specs=placed, out_specs=P("row", ("grp", "frm"), None), check_vma=False
    )
```

```python
import jax
import jax.numpy as jnp
from jax import lax
from jax.experimental import pallas as pl
from jax.experimental.pallas import tpu as pltpu
from jax.sharding import PartitionSpec as P


HD = 112
EPS = 1e-06
F32 = jnp.float32
BF16 = jnp.bfloat16


def cost(flops, nbytes):
    return pl.CostEstimate(flops=int(flops), bytes_accessed=int(nbytes), transcendentals=0)


def params(mib=24):
    return pltpu.CompilerParams(vmem_limit_bytes=mib << 20)


def dot(a, b):
    return jnp.dot(a, b, preferred_element_type=F32)


def dot_nt(a, b):
    return lax.dot_general(a, b, (((1,), (1,)), ((), ())), preferred_element_type=F32)


VMEM = pl.BlockSpec(memory_space=pltpu.VMEM)


def scaled(x_ref, gain_ref):
    x = x_ref[...].astype(F32)
    mean = jnp.mean(x * x, axis=0, keepdims=True)
    return (x * lax.rsqrt(mean + EPS) * gain_ref[...]).astype(BF16)


def project(blocks, where, gain, weights, states=None, frames=1, first=0, with_query=True, last=False):
    n = len(blocks)
    here, per_frame = len(where), len(where[0])
    features, lanes = blocks[0].shape[-2:]
    group = weights.shape[0] // 3
    heads = group // HD
    width = per_frame * lanes
    total = here * width
    begin = 0 if with_query else group

    def kernel(*refs):
        x_refs, rest = refs[:n], refs[n:]
        gain_ref, w_ref, rest = rest[0], rest[1], rest[2:]
        if states is not None:
            old, rest = rest[0], rest[1:]
        state, second, normed, part = rest[0], rest[1], rest[-2], rest[-1]
        for f in range(here):
            for b, (k, i) in enumerate(where[f]):
                block = x_refs[k] if i is None else x_refs[k].at[i]
                at = f * width + b * lanes
                normed[:, at : at + lanes] = scaled(block, gain_ref)
        part[...] = jnp.dot(w_ref[begin:, :], normed[...], preferred_element_type=F32).astype(BF16)
        keys, values = group - begin, 2 * group - begin
        for f in range(here):
            cols = slice(f * width, (f + 1) * width)
            for h in range(heads):
                k = jnp.maximum(part[keys + h * HD : keys + (h + 1) * HD, cols], 0.0)
                v = part[values + h * HD : values + (h + 1) * HD, cols]
                rows = slice(h * HD, (h + 1) * HD)
                add = dot_nt(v, k)
                state[first + f, rows, :] = add if states is None else old[first + f, rows, :] + add
        if states is not None:
            for f in range(frames):
                if not first <= f < first + here:
                    state[f] = old[f]
        if last:
            own = state[0]
            for f in range(1, frames):
                own = own + state[f]
            second[...] = own.astype(BF16)
        if with_query:
            for f in range(here):
                second[f] = jnp.maximum(part[:group, f * width : (f + 1) * width], 0.0)

    out_shape = [jax.ShapeDtypeStruct((frames, group, HD), F32)]
    scratch = [pltpu.VMEM((3 * group - begin, total), BF16)]
    if last:
        out_shape.append(jax.ShapeDtypeStruct((group, HD), BF16))
    if not with_query:
        out_shape.append(jax.ShapeDtypeStruct((features, total), BF16))
    else:
        out_shape.append(jax.ShapeDtypeStruct((here, group, width), BF16))
        scratch = [pltpu.VMEM((features, total), BF16)] + scratch
    given = [*blocks, gain, weights] + ([] if states is None else [states])
    return pl.pallas_call(
        kernel,
        in_specs=[VMEM] * len(given),
        out_specs=[VMEM] * len(out_shape),
        out_shape=out_shape,
        scratch_shapes=scratch,
        compiler_params=params(),
        cost_estimate=cost(2 * (3 * group - begin) * features * total, 2 * features * total),
        name="project",
    )(*given)


def query(normed, weights, frames):
    features, total = normed.shape
    group = weights.shape[0] // 3
    width = total // frames

    def kernel(x_ref, w_ref, q_ref):
        q = jnp.maximum(dot(w_ref[:group, :], x_ref[...]), 0.0).astype(BF16)
        for f in range(frames):
            q_ref[f] = q[:, f * width : (f + 1) * width]

    return pl.pallas_call(
        kernel,
        in_specs=[VMEM] * 2,
        out_specs=VMEM,
        out_shape=jax.ShapeDtypeStruct((frames, group, width), BF16),
        compiler_params=params(),
        cost_estimate=cost(2 * group * features * total, 2 * features * total),
        name="query",
    )(normed, weights)


def attend(end, states, priors, head_gain, queries, lanes):
    frames, group, _ = states.shape
    heads = group // HD
    n_prior, n_q = len(priors), len(queries)
    places, slabs = [], 0
    seen = {}
    for k, (array, where, first) in enumerate(queries):
        for f, i in where.items():
            for b in range(array.shape[-1] // lanes):
                places.append((k, f, i, b, first + b))
                seen[first + b] = True
    slabs = len(seen)

    def kernel(end_ref, state_ref, gain_ref, *rest):
        prior_refs, q_refs = rest[:n_prior], rest[n_prior : n_prior + n_q]
        outs = rest[n_prior + n_q :]
        prior = jnp.zeros((group, HD), F32)
        for p in prior_refs:
            prior = prior + p[...].astype(F32)
        block = []
        for f in range(frames):
            total = prior
            for g in range(frames):
                seen_by = (end_ref[g] <= end_ref[f]).astype(F32)
                total = total + seen_by * state_ref[g]
            block.append(total.astype(BF16))
        for k, f, i, b, slab in places:
            for h in range(heads):
                rows = slice(h * HD, (h + 1) * HD)
                a = dot(block[f][rows], q_refs[k][i, rows, b * lanes : (b + 1) * lanes])
                mean = jnp.mean(a * a, axis=0, keepdims=True)
                outs[slab][f, rows, :] = (a * lax.rsqrt(mean + EPS) * gain_ref[rows]).astype(BF16)

    return pl.pallas_call(
        kernel,
        in_specs=[pl.BlockSpec(memory_space=pltpu.SMEM)]
        + [pl.BlockSpec(memory_space=pltpu.VMEM)] * (2 + n_prior + n_q),
        out_specs=[pl.BlockSpec(memory_space=pltpu.VMEM)] * slabs,
        out_shape=[jax.ShapeDtypeStruct((frames, group, lanes), BF16)] * slabs,
        compiler_params=params(),
        cost_estimate=cost(2 * group * HD * frames * slabs * lanes, 4 * group * frames * slabs * lanes),
        name="attend",
    )(end, states, head_gain, *priors, *[a for a, _, _ in queries])


def cut(source, start, sizes):
    width = source.shape[-1]

    def kernel(start_ref, src, *rest):
        outs, sem = rest[: len(sizes)], rest[-1]
        copies, at = [], 0
        for k, (out, n) in enumerate(zip(outs, sizes)):
            view = src.at[pl.ds(pl.multiple_of(start_ref[0] + at, 8), n), :]
            copies.append(pltpu.make_async_copy(view, out, sem.at[k]))
            copies[-1].start()
            at += n
        for c in copies:
            c.wait()

    return pl.pallas_call(
        kernel,
        in_specs=[pl.BlockSpec(memory_space=pltpu.SMEM), pl.BlockSpec(memory_space=pl.ANY)],
        out_specs=[VMEM] * len(sizes),
        out_shape=[jax.ShapeDtypeStruct((n, width), source.dtype) for n in sizes],
        scratch_shapes=[pltpu.SemaphoreType.DMA((len(sizes),))],
        compiler_params=params(8),
        cost_estimate=cost(0, 4 * sum(sizes) * width),
        name="cut",
    )(start.reshape(1), source)


def tokens_first(ref):
    return jnp.concatenate([ref[f].T for f in range(ref.shape[0])], axis=0)


def mix(rows, heads_out):
    frames, group, lanes = heads_out[0].shape
    width = rows[0].shape[1]
    n = len(rows)

    def kernel(*refs):
        out = refs[2 * n]
        total = None
        for w, x in zip(refs[:n], refs[n : 2 * n]):
            term = dot(tokens_first(x), w[...])
            total = term if total is None else total + term
        out[...] = total

    return pl.pallas_call(
        kernel,
        in_specs=[VMEM] * (2 * n),
        out_specs=VMEM,
        out_shape=jax.ShapeDtypeStruct((frames * lanes, width), F32),
        compiler_params=params(),
        cost_estimate=cost(4 * width * group * frames * lanes, 4 * width * group),
        name="mix",
    )(*rows, *heads_out)


def copy_rows(refs, matrix, sem, at=0):
    copies = []
    for i, ref in enumerate(refs):
        copies.append(pltpu.make_async_copy(ref, matrix.at[pl.ds(at, ref.shape[0]), :], sem.at[i]))
        copies[-1].start()
        at += ref.shape[0]
    return copies


def add_heads(index, total, parts, shares, matrix=None, ahead=(), room=0):
    heads = []
    for h, _, _, _ in parts:
        if not any(h is other for other in heads):
            heads.append(h)
    frames, group, lanes = heads[0].shape
    share = group // shares
    width = total.shape[1]
    which = [next(i for i, other in enumerate(heads) if other is h) for h, _, _, _ in parts]
    given = [p for _, _, _, pieces in parts for p in pieces]
    given = given if matrix is None else [matrix, given[-1]]
    n, m, n_ahead = len(given), len(heads), len(ahead)
    depth = sum(p.shape[0] for _, _, _, pieces in parts for p in pieces)
    step = 640 if width > 640 else width
    spans = [(a, min(a + step, width)) for a in range(0, width, step)]

    def kernel(index_ref, total_ref, *refs):
        head_refs, piece_refs, refs = refs[:m], refs[m : m + n], refs[m + n :]
        next_refs, out, scratch = refs[:n_ahead], refs[n_ahead], refs[n_ahead + 1 :]
        w = scratch[0] if matrix is not None else scratch[-2]
        if matrix is None:
            waits = copy_rows(piece_refs, w, scratch[-1])
        else:
            waits = copy_rows(piece_refs[1:], w, scratch[-1], depth - given[1].shape[0])
        coming = copy_rows(next_refs, scratch[0], scratch[1]) if ahead else []
        left = []
        for f in range(frames):
            rows = []
            for k, (_, g, first, pieces) in zip(which, parts):
                count = sum(p.shape[0] for p in pieces)
                got = head_refs[k][f, first : first + count, :]
                for t in range(1, shares):
                    there = t * share + first
                    got = jnp.where(index_ref[g] == t, head_refs[k][f, there : there + count, :], got)
                rows.append(got)
            left.append(jnp.concatenate(rows, axis=0).T)
        left = jnp.concatenate(left, axis=0)
        for c in waits:
            c.wait()
        for a, b in spans:
            out[:, a:b] = total_ref[:, a:b] + dot(left, w[:, a:b])
        for c in coming:
            c.wait()

    results, places = [jax.ShapeDtypeStruct(total.shape, F32)], [VMEM]
    scratch = []
    if ahead:
        results.append(pltpu.VMEM((room, width), BF16))
        places.append(VMEM)
        scratch.append(pltpu.SemaphoreType.DMA((n_ahead,)))
    if matrix is not None:
        results.append(pltpu.VMEM(matrix.shape, BF16))
        places.append(VMEM)
        scratch.append(pltpu.SemaphoreType.DMA((1,)))
    else:
        scratch += [pltpu.VMEM((depth, width), BF16), pltpu.SemaphoreType.DMA((n,))]
    anywhere = pl.BlockSpec(memory_space=pl.ANY)
    out = pl.pallas_call(
        kernel,
        in_specs=[pl.BlockSpec(memory_space=pltpu.SMEM)]
        + [VMEM] * (1 + m)
        + [VMEM if v is matrix else anywhere for v in given]
        + [anywhere] * n_ahead,
        out_specs=places,
        out_shape=results,
        scratch_shapes=scratch,
        input_output_aliases={} if matrix is None else {2 + m: 1},
        compiler_params=params(),
        cost_estimate=cost(2 * depth * width * frames * lanes, 2 * depth * width),
        name="add_heads",
    )(index, total, *heads, *given, *ahead)
    return out if ahead else out[0]


def add_last(index, total, parts, shares):
    heads = []
    for h, _, _, _ in parts:
        if not any(h is other for other in heads):
            heads.append(h)
    frames, group, lanes = heads[0].shape
    share = group // shares
    width = total.shape[1]
    which = [next(i for i, other in enumerate(heads) if other is h) for h, _, _, _ in parts]
    given = [p for _, _, _, pieces in parts for p in pieces]
    n, m = len(given), len(heads)
    depth = sum(p.shape[0] for p in given)
    step = 640 if width > 640 else width
    spans = [(a, min(a + step, width)) for a in range(0, width, step)]

    def kernel(index_ref, total_ref, *refs):
        head_refs, piece_refs, (out, w, staged, sem) = refs[:m], refs[m : m + n], refs[m + n :]
        at = 0
        for ref in piece_refs:
            w[at : at + ref.shape[0], :] = ref[...]
            at += ref.shape[0]
        copies = []
        for f in range(frames):
            rows = []
            for k, (_, g, first, pieces) in zip(which, parts):
                count = sum(p.shape[0] for p in pieces)
                got = head_refs[k][f, first : first + count, :]
                for t in range(1, shares):
                    there = t * share + first
                    got = jnp.where(index_ref[g] == t, head_refs[k][f, there : there + count, :], got)
                rows.append(got)
            left = jnp.concatenate(rows, axis=0).T
            here = slice(f * lanes, (f + 1) * lanes)
            for a, b in spans:
                term = total_ref[here, a:b] + dot(left, w[:, a:b])
                staged[f, a:b, :] = term.T.astype(BF16)
            copies.append(pltpu.make_async_copy(staged.at[f], out.at[f], sem.at[f]))
            copies[-1].start()
        for c in copies:
            c.wait()

    shape = (frames, width, lanes)
    return pl.pallas_call(
        kernel,
        in_specs=[pl.BlockSpec(memory_space=pltpu.SMEM)] + [VMEM] * (1 + m + n),
        out_specs=pl.BlockSpec(memory_space=pl.ANY),
        out_shape=jax.ShapeDtypeStruct(shape, BF16),
        scratch_shapes=[
            pltpu.VMEM((depth, width), BF16),
            pltpu.VMEM(shape, BF16),
            pltpu.SemaphoreType.DMA((frames,)),
        ],
        compiler_params=params(),
        cost_estimate=cost(2 * depth * width * frames * lanes, 2 * depth * width),
        name="add_last",
    )(index, total, *heads, *given)


CUTS = (0, 11, 24, 32)
PIECES = len(CUTS) - 1


def per_device(n_grp, n_row, n_frm, hidden_in, norm_gain, qkv_weight, head_gain, output_matrix, block_end):
    def swap(v, k, axis="row"):
        size = {"row": n_row, "grp": n_grp}[axis]
        return lax.ppermute(v, axis, [(i, i ^ k) for i in range(size)])

    def shift(v, s):
        return lax.ppermute(v, "frm", [(i, i + s) for i in range(n_frm - s)])

    lanes, frames, features = hidden_in.shape
    tokens = jnp.transpose(hidden_in, (1, 2, 0))
    weights = jnp.transpose(qkv_weight, (1, 2, 0)).reshape(-1, features)
    gain = norm_gain.reshape(features, 1)
    out_gain = head_gain.reshape(-1, 1)

    pairs = n_row // 2
    crossed = {k: swap(tokens, 2 * k) for k in range(1, pairs)}
    sibling = swap(tokens, 1)
    passed = {k: swap(v, 1) for k, v in crossed.items()}

    where = [[(0, f), (1, f)] for f in range(frames)]
    states, near_q = project([tokens, sibling], where, gain, weights, None, frames)


    group, _ = output_matrix.shape
    grp = lax.axis_index("grp")
    share = group // n_grp
    sizes = [8 * (share // 8 * b // 32 - share // 8 * a // 32) for a, b in zip(CUTS[:-1], CUTS[1:])]
    pieces = cut(output_matrix, grp * share, sizes)
    near_rows = swap(output_matrix, 1)
    index = jnp.stack([grp ^ g for g in range(n_grp)])
    far_rows = []
    for k in range(1, pairs):
        held = {}
        for j, piece in enumerate(pieces):
            held[0, 0, j] = swap(piece, 2 * k)
            for g in range(1, n_grp):
                held[0, g, j] = swap(held[0, 0, j], g, "grp")
            for g in range(n_grp):
                held[1, g, j] = swap(held[0, g, j], 1)
        far_rows.append(held)
    queries = [(near_q, {f: f for f in range(frames)}, 0)]
    waiting = []
    for k in range(1, pairs):
        for c, block in enumerate((crossed[k], passed[k])):
            last = c == 1 and k == pairs - 1
            one = [[(0, f)] for f in range(frames)]
            out = project([block], one, gain, weights, states, frames, 0, False, last)
            states = out[0]
            if last:
                own_sum = out[1]
            waiting.append((out[-1], 2 * k + c))
    if n_frm <= 4:
        priors = [shift(own_sum, s) for s in range(1, n_frm)]
    else:
        total, s = shift(own_sum.astype(F32), 1), 1
        while s < n_frm:
            total, s = total + shift(total, s), 2 * s
        priors = [total]
    for normed, slab in waiting:
        late = query(normed, weights, frames)
        queries.append((late, {f: f for f in range(frames)}, slab))
    heads_out = attend(block_end, states, priors, out_gain, queries, lanes)

    across = []
    for k in range(1, pairs):
        across.append((swap(heads_out[2 * k], 2 * k), swap(heads_out[2 * k + 1], 2 * k + 1)))
    own = mix([output_matrix, near_rows], [heads_out[0], swap(heads_out[1], 1)])
    total, late = own, sum(sizes[:-1])
    for k, (heads, held) in enumerate(zip(across, far_rows)):
        parts = []
        for c in range(2):
            parts.append([(heads[c], 0, 0, [held[c, 0, j] for j in range(PIECES)])])
            parts[c] += [(heads[c], g, 0, [held[c, g, j] for j in range(PIECES - 1)]) for g in range(1, n_grp)]
        ahead = [p for _, _, _, pieces in parts[1] for p in pieces]
        room = sum(p.shape[0] for p in ahead)
        total, matrix = add_heads(index, total, parts[0], n_grp, None, ahead[:-1], room)
        total = add_heads(index, total, parts[1], n_grp, matrix)
        parts = [(heads[c], g, late, [held[c, g, PIECES - 1]]) for c in range(2) for g in range(1, n_grp)]
        if k == pairs - 2:
            total = add_last(index, total, parts, n_grp)
        else:
            total = add_heads(index, total, parts, n_grp)
    return jnp.transpose(total, (2, 0, 1))


def solution(mesh):
    placed = (
        P("row", ("grp", "frm"), None),
        P(),
        P(None, None, "row"),
        P("row"),
        P("row", None),
        P(("grp", "frm")),
    )

    def body(*args):
        return per_device(mesh.shape["grp"], mesh.shape["row"], mesh.shape["frm"], *args)

    return jax.shard_map(
        body, mesh=mesh, in_specs=placed, out_specs=P("row", ("grp", "frm"), None), check_vma=False
    )
```

```python
import jax
import jax.numpy as jnp
from jax import lax
from jax.experimental import pallas as pl
from jax.experimental.pallas import tpu as pltpu
from jax.sharding import PartitionSpec as P


HD = 112
EPS = 1e-06
F32 = jnp.float32
BF16 = jnp.bfloat16


def cost(flops, nbytes):
    return pl.CostEstimate(flops=int(flops), bytes_accessed=int(nbytes), transcendentals=0)


def params(mib=24):
    return pltpu.CompilerParams(vmem_limit_bytes=mib << 20)


def dot(a, b):
    return jnp.dot(a, b, preferred_element_type=F32)


def dot_nt(a, b):
    return lax.dot_general(a, b, (((1,), (1,)), ((), ())), preferred_element_type=F32)


VMEM = pl.BlockSpec(memory_space=pltpu.VMEM)


def scaled(x_ref, gain_ref):
    x = x_ref[...].astype(F32)
    mean = jnp.mean(x * x, axis=0, keepdims=True)
    return (x * lax.rsqrt(mean + EPS) * gain_ref[...]).astype(BF16)


def project(blocks, where, gain, weights, states=None, frames=1, first=0, with_query=True, last=False):
    n = len(blocks)
    here, per_frame = len(where), len(where[0])
    features, lanes = blocks[0].shape[-2:]
    group = weights.shape[0] // 3
    heads = group // HD
    width = per_frame * lanes
    total = here * width
    begin = 0 if with_query else group

    def kernel(*refs):
        x_refs, rest = refs[:n], refs[n:]
        gain_ref, w_ref, rest = rest[0], rest[1], rest[2:]
        if states is not None:
            old, rest = rest[0], rest[1:]
        state, second, normed, part = rest[0], rest[1], rest[-2], rest[-1]
        for f in range(here):
            for b, (k, i) in enumerate(where[f]):
                block = x_refs[k] if i is None else x_refs[k].at[i]
                at = f * width + b * lanes
                normed[:, at : at + lanes] = scaled(block, gain_ref)
        part[...] = jnp.dot(w_ref[begin:, :], normed[...], preferred_element_type=F32).astype(BF16)
        keys, values = group - begin, 2 * group - begin
        for f in range(here):
            cols = slice(f * width, (f + 1) * width)
            for h in range(heads):
                k = jnp.maximum(part[keys + h * HD : keys + (h + 1) * HD, cols], 0.0)
                v = part[values + h * HD : values + (h + 1) * HD, cols]
                rows = slice(h * HD, (h + 1) * HD)
                add = dot_nt(v, k)
                state[first + f, rows, :] = add if states is None else old[first + f, rows, :] + add
        if states is not None:
            for f in range(frames):
                if not first <= f < first + here:
                    state[f] = old[f]
        if last:
            own = state[0]
            for f in range(1, frames):
                own = own + state[f]
            second[...] = own.astype(BF16)
        if with_query:
            for f in range(here):
                second[f] = jnp.maximum(part[:group, f * width : (f + 1) * width], 0.0)

    out_shape = [jax.ShapeDtypeStruct((frames, group, HD), F32)]
    scratch = [pltpu.VMEM((3 * group - begin, total), BF16)]
    if last:
        out_shape.append(jax.ShapeDtypeStruct((group, HD), BF16))
    if not with_query:
        out_shape.append(jax.ShapeDtypeStruct((features, total), BF16))
    else:
        out_shape.append(jax.ShapeDtypeStruct((here, group, width), BF16))
        scratch = [pltpu.VMEM((features, total), BF16)] + scratch
    given = [*blocks, gain, weights] + ([] if states is None else [states])
    return pl.pallas_call(
        kernel,
        in_specs=[VMEM] * len(given),
        out_specs=[VMEM] * len(out_shape),
        out_shape=out_shape,
        scratch_shapes=scratch,
        compiler_params=params(),
        cost_estimate=cost(2 * (3 * group - begin) * features * total, 2 * features * total),
        name="project",
    )(*given)


def query(normed, weights, frames):
    features, total = normed.shape
    group = weights.shape[0] // 3
    width = total // frames

    def kernel(x_ref, w_ref, q_ref):
        q = jnp.maximum(dot(w_ref[:group, :], x_ref[...]), 0.0).astype(BF16)
        for f in range(frames):
            q_ref[f] = q[:, f * width : (f + 1) * width]

    return pl.pallas_call(
        kernel,
        in_specs=[VMEM] * 2,
        out_specs=VMEM,
        out_shape=jax.ShapeDtypeStruct((frames, group, width), BF16),
        compiler_params=params(),
        cost_estimate=cost(2 * group * features * total, 2 * features * total),
        name="query",
    )(normed, weights)


def attend(end, states, priors, head_gain, queries, lanes):
    frames, group, _ = states.shape
    heads = group // HD
    n_prior, n_q = len(priors), len(queries)
    places, slabs = [], 0
    seen = {}
    for k, (array, where, first) in enumerate(queries):
        for f, i in where.items():
            for b in range(array.shape[-1] // lanes):
                places.append((k, f, i, b, first + b))
                seen[first + b] = True
    slabs = len(seen)

    def kernel(end_ref, state_ref, gain_ref, *rest):
        prior_refs, q_refs = rest[:n_prior], rest[n_prior : n_prior + n_q]
        outs = rest[n_prior + n_q :]
        prior = jnp.zeros((group, HD), F32)
        for p in prior_refs:
            prior = prior + p[...].astype(F32)
        block = []
        for f in range(frames):
            total = prior
            for g in range(frames):
                seen_by = (end_ref[g] <= end_ref[f]).astype(F32)
                total = total + seen_by * state_ref[g]
            block.append(total.astype(BF16))
        for k, f, i, b, slab in places:
            for h in range(heads):
                rows = slice(h * HD, (h + 1) * HD)
                a = dot(block[f][rows], q_refs[k][i, rows, b * lanes : (b + 1) * lanes])
                mean = jnp.mean(a * a, axis=0, keepdims=True)
                outs[slab][f, rows, :] = (a * lax.rsqrt(mean + EPS) * gain_ref[rows]).astype(BF16)

    return pl.pallas_call(
        kernel,
        in_specs=[pl.BlockSpec(memory_space=pltpu.SMEM)]
        + [pl.BlockSpec(memory_space=pltpu.VMEM)] * (2 + n_prior + n_q),
        out_specs=[pl.BlockSpec(memory_space=pltpu.VMEM)] * slabs,
        out_shape=[jax.ShapeDtypeStruct((frames, group, lanes), BF16)] * slabs,
        compiler_params=params(),
        cost_estimate=cost(2 * group * HD * frames * slabs * lanes, 4 * group * frames * slabs * lanes),
        name="attend",
    )(end, states, head_gain, *priors, *[a for a, _, _ in queries])


def cut(source, start, sizes):
    width = source.shape[-1]

    def kernel(start_ref, src, *rest):
        outs, sem = rest[: len(sizes)], rest[-1]
        copies, at = [], 0
        for k, (out, n) in enumerate(zip(outs, sizes)):
            view = src.at[pl.ds(pl.multiple_of(start_ref[0] + at, 8), n), :]
            copies.append(pltpu.make_async_copy(view, out, sem.at[k]))
            copies[-1].start()
            at += n
        for c in copies:
            c.wait()

    return pl.pallas_call(
        kernel,
        in_specs=[pl.BlockSpec(memory_space=pltpu.SMEM), pl.BlockSpec(memory_space=pl.ANY)],
        out_specs=[VMEM] * len(sizes),
        out_shape=[jax.ShapeDtypeStruct((n, width), source.dtype) for n in sizes],
        scratch_shapes=[pltpu.SemaphoreType.DMA((len(sizes),))],
        compiler_params=params(8),
        cost_estimate=cost(0, 4 * sum(sizes) * width),
        name="cut",
    )(start.reshape(1), source)


def tokens_first(ref):
    return jnp.concatenate([ref[f].T for f in range(ref.shape[0])], axis=0)


def mix(rows, heads_out):
    frames, group, lanes = heads_out[0].shape
    width = rows[0].shape[1]
    n = len(rows)

    def kernel(*refs):
        out = refs[2 * n]
        total = None
        for w, x in zip(refs[:n], refs[n : 2 * n]):
            term = dot(tokens_first(x), w[...])
            total = term if total is None else total + term
        out[...] = total

    return pl.pallas_call(
        kernel,
        in_specs=[VMEM] * (2 * n),
        out_specs=VMEM,
        out_shape=jax.ShapeDtypeStruct((frames * lanes, width), F32),
        compiler_params=params(),
        cost_estimate=cost(4 * width * group * frames * lanes, 4 * width * group),
        name="mix",
    )(*rows, *heads_out)


def copy_rows(refs, matrix, sem):
    copies, at = [], 0
    for i, ref in enumerate(refs):
        copies.append(pltpu.make_async_copy(ref, matrix.at[pl.ds(at, ref.shape[0]), :], sem.at[i]))
        copies[-1].start()
        at += ref.shape[0]
    return copies


def add_heads(index, total, parts, shares, matrix=None, ahead=()):
    heads = []
    for h, _, _, _ in parts:
        if not any(h is other for other in heads):
            heads.append(h)
    frames, group, lanes = heads[0].shape
    share = group // shares
    width = total.shape[1]
    which = [next(i for i, other in enumerate(heads) if other is h) for h, _, _, _ in parts]
    given = [p for _, _, _, pieces in parts for p in pieces] if matrix is None else [matrix]
    n, m, n_ahead = len(given), len(heads), len(ahead)
    depth = sum(p.shape[0] for p in given)
    step = 640 if width > 640 else width
    spans = [(a, min(a + step, width)) for a in range(0, width, step)]

    def kernel(index_ref, total_ref, *refs):
        head_refs, piece_refs, refs = refs[:m], refs[m : m + n], refs[m + n :]
        next_refs, out, scratch = refs[:n_ahead], refs[n_ahead], refs[n_ahead + 1 :]
        w = piece_refs[0] if matrix is not None else scratch[-2]
        waits = []
        if matrix is None:
            waits = copy_rows(piece_refs, w, scratch[-1])
        coming = copy_rows(next_refs, scratch[0], scratch[1]) if ahead else []
        left = []
        for f in range(frames):
            rows = []
            for k, (_, g, first, pieces) in zip(which, parts):
                count = sum(p.shape[0] for p in pieces)
                got = head_refs[k][f, first : first + count, :]
                for t in range(1, shares):
                    there = t * share + first
                    got = jnp.where(index_ref[g] == t, head_refs[k][f, there : there + count, :], got)
                rows.append(got)
            left.append(jnp.concatenate(rows, axis=0).T)
        left = jnp.concatenate(left, axis=0)
        for c in waits:
            c.wait()
        for a, b in spans:
            out[:, a:b] = total_ref[:, a:b] + dot(left, w[:, a:b])
        for c in coming:
            c.wait()

    results, places = [jax.ShapeDtypeStruct(total.shape, F32)], [VMEM]
    scratch = []
    if ahead:
        results.append(pltpu.VMEM((sum(p.shape[0] for p in ahead), width), BF16))
        places.append(VMEM)
        scratch.append(pltpu.SemaphoreType.DMA((n_ahead,)))
    if matrix is None:
        scratch += [pltpu.VMEM((depth, width), BF16), pltpu.SemaphoreType.DMA((n,))]
    anywhere = pl.BlockSpec(memory_space=pl.ANY)
    out = pl.pallas_call(
        kernel,
        in_specs=[pl.BlockSpec(memory_space=pltpu.SMEM)]
        + [VMEM] * (1 + m)
        + [anywhere if matrix is None else VMEM] * n
        + [anywhere] * n_ahead,
        out_specs=places,
        out_shape=results,
        scratch_shapes=scratch,
        compiler_params=params(),
        cost_estimate=cost(2 * depth * width * frames * lanes, 2 * depth * width),
        name="add_heads",
    )(index, total, *heads, *given, *ahead)
    return out if ahead else out[0]


def add_last(index, total, parts, shares):
    heads = []
    for h, _, _, _ in parts:
        if not any(h is other for other in heads):
            heads.append(h)
    frames, group, lanes = heads[0].shape
    share = group // shares
    width = total.shape[1]
    which = [next(i for i, other in enumerate(heads) if other is h) for h, _, _, _ in parts]
    given = [p for _, _, _, pieces in parts for p in pieces]
    n, m = len(given), len(heads)
    depth = sum(p.shape[0] for p in given)
    step = 640 if width > 640 else width
    spans = [(a, min(a + step, width)) for a in range(0, width, step)]

    def kernel(index_ref, total_ref, *refs):
        head_refs, piece_refs, (out, w, staged, sem) = refs[:m], refs[m : m + n], refs[m + n :]
        at = 0
        for ref in piece_refs:
            w[at : at + ref.shape[0], :] = ref[...]
            at += ref.shape[0]
        copies = []
        for f in range(frames):
            rows = []
            for k, (_, g, first, pieces) in zip(which, parts):
                count = sum(p.shape[0] for p in pieces)
                got = head_refs[k][f, first : first + count, :]
                for t in range(1, shares):
                    there = t * share + first
                    got = jnp.where(index_ref[g] == t, head_refs[k][f, there : there + count, :], got)
                rows.append(got)
            left = jnp.concatenate(rows, axis=0).T
            here = slice(f * lanes, (f + 1) * lanes)
            for a, b in spans:
                term = total_ref[here, a:b] + dot(left, w[:, a:b])
                staged[f, a:b, :] = term.astype(BF16).T
            copies.append(pltpu.make_async_copy(staged.at[f], out.at[f], sem.at[f]))
            copies[-1].start()
        for c in copies:
            c.wait()

    shape = (frames, width, lanes)
    return pl.pallas_call(
        kernel,
        in_specs=[pl.BlockSpec(memory_space=pltpu.SMEM)] + [VMEM] * (1 + m + n),
        out_specs=pl.BlockSpec(memory_space=pl.ANY),
        out_shape=jax.ShapeDtypeStruct(shape, BF16),
        scratch_shapes=[
            pltpu.VMEM((depth, width), BF16),
            pltpu.VMEM(shape, BF16),
            pltpu.SemaphoreType.DMA((frames,)),
        ],
        compiler_params=params(),
        cost_estimate=cost(2 * depth * width * frames * lanes, 2 * depth * width),
        name="add_last",
    )(index, total, *heads, *given)


CUTS = (0, 11, 22, 32)
PIECES = len(CUTS) - 1


def per_device(n_grp, n_row, n_frm, hidden_in, norm_gain, qkv_weight, head_gain, output_matrix, block_end):
    def swap(v, k, axis="row"):
        size = {"row": n_row, "grp": n_grp}[axis]
        return lax.ppermute(v, axis, [(i, i ^ k) for i in range(size)])

    def shift(v, s):
        return lax.ppermute(v, "frm", [(i, i + s) for i in range(n_frm - s)])

    lanes, frames, features = hidden_in.shape
    tokens = jnp.transpose(hidden_in, (1, 2, 0))
    weights = jnp.transpose(qkv_weight, (1, 2, 0)).reshape(-1, features)
    gain = norm_gain.reshape(features, 1)
    out_gain = head_gain.reshape(-1, 1)

    pairs = n_row // 2
    crossed = {k: swap(tokens, 2 * k) for k in range(1, pairs)}
    sibling = swap(tokens, 1)
    passed = {k: swap(v, 1) for k, v in crossed.items()}

    where = [[(0, f), (1, f)] for f in range(frames)]
    states, near_q = project([tokens, sibling], where, gain, weights, None, frames)


    group, _ = output_matrix.shape
    grp = lax.axis_index("grp")
    share = group // n_grp
    sizes = [8 * (share // 8 * b // 32 - share // 8 * a // 32) for a, b in zip(CUTS[:-1], CUTS[1:])]
    pieces = cut(output_matrix, grp * share, sizes)
    near_rows = swap(output_matrix, 1)
    index = jnp.stack([grp ^ g for g in range(n_grp)])
    far_rows = []
    for k in range(1, pairs):
        held = {}
        for j, piece in enumerate(pieces):
            held[0, 0, j] = swap(piece, 2 * k)
            for g in range(1, n_grp):
                held[0, g, j] = swap(held[0, 0, j], g, "grp")
            for g in range(n_grp):
                held[1, g, j] = swap(held[0, g, j], 1)
        far_rows.append(held)
    queries = [(near_q, {f: f for f in range(frames)}, 0)]
    waiting = []
    for k in range(1, pairs):
        for c, block in enumerate((crossed[k], passed[k])):
            last = c == 1 and k == pairs - 1
            one = [[(0, f)] for f in range(frames)]
            out = project([block], one, gain, weights, states, frames, 0, False, last)
            states = out[0]
            if last:
                own_sum = out[1]
            waiting.append((out[-1], 2 * k + c))
    if n_frm <= 4:
        priors = [shift(own_sum, s) for s in range(1, n_frm)]
    else:
        total, s = shift(own_sum.astype(F32), 1), 1
        while s < n_frm:
            total, s = total + shift(total, s), 2 * s
        priors = [total]
    for normed, slab in waiting:
        late = query(normed, weights, frames)
        queries.append((late, {f: f for f in range(frames)}, slab))
    heads_out = attend(block_end, states, priors, out_gain, queries, lanes)

    across = []
    for k in range(1, pairs):
        across.append((swap(heads_out[2 * k], 2 * k), swap(heads_out[2 * k + 1], 2 * k + 1)))
    own = mix([output_matrix, near_rows], [heads_out[0], swap(heads_out[1], 1)])
    total, late = own, sum(sizes[:-1])
    for k, (heads, held) in enumerate(zip(across, far_rows)):
        parts = []
        for c in range(2):
            parts.append([(heads[c], 0, 0, [held[c, 0, j] for j in range(PIECES)])])
            parts[c] += [(heads[c], g, 0, [held[c, g, j] for j in range(PIECES - 1)]) for g in range(1, n_grp)]
        ahead = [p for _, _, _, pieces in parts[1] for p in pieces]
        total, matrix = add_heads(index, total, parts[0], n_grp, None, ahead)
        total = add_heads(index, total, parts[1], n_grp, matrix)
        parts = [(heads[c], g, late, [held[c, g, PIECES - 1]]) for c in range(2) for g in range(1, n_grp)]
        if k == pairs - 2:
            total = add_last(index, total, parts, n_grp)
        else:
            total = add_heads(index, total, parts, n_grp)
    return jnp.transpose(total, (2, 0, 1))


def solution(mesh):
    placed = (
        P("row", ("grp", "frm"), None),
        P(),
        P(None, None, "row"),
        P("row"),
        P("row", None),
        P(("grp", "frm")),
    )

    def body(*args):
        return per_device(mesh.shape["grp"], mesh.shape["row"], mesh.shape["frm"], *args)

    return jax.shard_map(
        body, mesh=mesh, in_specs=placed, out_specs=P("row", ("grp", "frm"), None), check_vma=False
    )
```
